512 devices in a mesh: wide: 64 (over y, z), narrow: 8 (over x, core).
Axes of the slice: x: 4, y: 4, z: 16, core: 2. Of those that a mesh axis runs over, the one named last changes fastest.
Arguments:
- panel: float32 [8, 16777216], P(None, ('wide', 'narrow')), may hold values from -0.25 to 0.25
- signs: int32 [16777216], P(('wide', 'narrow')), may hold values from -1 to 1, as said below
- samples: int32 [65536], P(('wide', 'narrow')), may hold values from 0 to 16777215, as said below
Outputs:
- sketch: float32 [8, 65536], P(None, ('wide', 'narrow'))
The draws below stay inside these ranges and needn't reach their ends.
Inputs may be any that keep to these rules, and one draw needn't show every extreme that they name: `signs`: every entry is +1 or -1. `samples`: for every k, entries 128 * k to 128 * (k + 1) - 1 are distinct, increasing, and lie among rows 32768 * k to 32768 * (k + 1) - 1.
All inputs are finite; a program needn't handle non-finite values.
Results may differ from the reference program's by a relative error of at most 0.000071.
Values sent between devices are 32-bit elements; how exact they have to be, the bound alone decides.
A program may use at most 64 MiB of HBM per device.

```python
import math
import jax
import jax.numpy as jnp

COLS = 8
ROWS_DEV = 32768
SAMP_DEV = 128
ROWS = 16777216
SAMPLES = 65536


def draw_signs(key, part):
    flips = jax.random.randint(key, (ROWS,), 0, 2)
    return (2 * flips - 1).astype(jnp.int32)


def draw_samples(key, part):
    blocks = SAMPLES // SAMP_DEV
    keys = jax.random.split(jax.random.fold_in(key, 7), blocks)

    def one_block(block_key):
        order = jax.random.permutation(block_key, ROWS_DEV)[:SAMP_DEV]
        return jnp.sort(order)
    chosen = jax.vmap(one_block)(keys)
    chosen = chosen.at[0, 0].set(0)
    chosen = chosen.at[blocks - 1, SAMP_DEV - 1].set(ROWS_DEV - 1)
    starts = (jnp.arange(blocks) * ROWS_DEV)[:, None]
    return (chosen + starts).reshape(SAMPLES).astype(jnp.int32)


def level_of(own_key, dims, pieces, smallest, largest):
    factor_of = 1.0
    for dim, shards_of in pieces:
        draws = jax.random.uniform(jax.random.fold_in(jax.random.fold_in(own_key, 6), dim), (shards_of,), jnp.float32, smallest / len(pieces), largest / len(pieces))
        factor_of = factor_of * jnp.repeat(jnp.exp(draws), dims[dim] // shards_of).reshape((-1,) + (1,) * (len(dims) - 1 - dim))
    return factor_of


def noise(key, extent, deviation, reach, cuts=(), held_as=jnp.bfloat16):
    entries = jax.random.normal(key, extent, jnp.float32) * deviation
    if len(cuts) > 0:
        entries = level_of(key, extent, cuts, -0.22, 0.18) * entries
    return jnp.clip(entries, min=-reach, max=reach).astype(held_as)


def setup_inputs(seed: int = 0) -> dict:
    streams_of = jax.random.split(jax.random.key(seed), 4)
    panel = noise(streams_of[0], (COLS, ROWS), 0.03125, 0.25, ((1, 512),), jnp.float32)
    signs = draw_signs(jax.random.fold_in(streams_of[3], 71), 0)
    samples = draw_samples(jax.random.fold_in(streams_of[3], 71), 0)
    return {"panel": panel, "signs": signs, "samples": samples}


def reference(panel, signs, samples):
    values = panel * signs.astype(jnp.float32)[None, :]
    total = values.shape[1]
    levels = total.bit_length() - 1
    for level in range(levels):
        half = 2 ** level
        shaped = values.reshape(COLS, total // (2 * half), 2, half)
        first = shaped[:, :, 0, :]
        second = shaped[:, :, 1, :]
        values = jnp.stack([first + second, first - second], axis=2).reshape(COLS, total)
    scale = 1.0 / math.sqrt(SAMPLES)
    return jnp.take(values, samples, axis=1) * jnp.float32(scale)
```

```python
import functools
import math

import jax
import jax.numpy as jnp
from jax import lax
from jax.experimental import pallas as pl
from jax.experimental.pallas import tpu as pltpu
from jax.sharding import PartitionSpec as P

MESH = pl.DeviceIdType.MESH
NX, NY, NZ, NC = 4, 4, 16, 2
LANES = 128
LAG = 6


def parity(value, bits):
    shift = 1
    while shift * 2 < bits:
        shift *= 2
    while shift >= 1:
        value = value ^ (value >> shift)
        shift //= 2
    return value & 1


def hadamard(rows, columns, bits):
    left = lax.broadcasted_iota(jnp.int32, (rows, columns), 0)
    right = lax.broadcasted_iota(jnp.int32, (rows, columns), 1)
    odd = parity(left & right & ((1 << bits) - 1), bits)
    return (1 - 2 * odd).astype(jnp.float32).astype(jnp.bfloat16)


def split(values):
    high = values.astype(jnp.bfloat16)
    low = (values - high.astype(jnp.float32)).astype(jnp.bfloat16)
    return high, low


def signed(odd, values):
    return jnp.where(odd == 0, values, -values)


def kernel(
    scale, panel, signs, samples, out,
    mixed, sent, came, table, idx_y, idx_x, idx_all, pick, part, zsum, zcame, rows_out, rows_in,
    x_send, x_recv, iz_send, iz_recv, iy_send, iy_recv, ix_send, ix_recv, ia_send, ia_recv,
    q_send, q_recv, z_send, z_recv, r_send, r_recv, local,
):
    wide = lax.axis_index("wide")
    narrow = lax.axis_index("narrow")
    y, z = wide // NZ, wide % NZ
    x, core = narrow // NC, narrow % NC
    role0 = core == 0
    p = jnp.where(role0, x, y)
    q = jnp.where(role0, y, x)
    outer = panel.shape[1] // LANES

    def device(dx, dy, dz, dc):
        return (dy * NZ + dz, dx * NC + dc)

    def by_role(dp, dq, dz):
        return device(jnp.where(role0, dp, dq), jnp.where(role0, dq, dp), dz, core)

    def remote(src, dst, send, recv, to):
        return pltpu.make_async_remote_copy(
            src_ref=src, dst_ref=dst, send_sem=send, recv_sem=recv, device_id=to, device_id_type=MESH
        )

    def wait_bytes(ref, sem):
        pltpu.make_async_copy(ref, ref, sem).wait()

    barrier = pltpu.get_barrier_semaphore()

    def greet(to):
        pl.semaphore_signal(barrier, inc=1, device_id=to, device_id_type=MESH)

    @pl.loop(1, NZ)
    def _(step):
        greet(device(x, y, lax.rem(z + step, NZ), core))

    @pl.loop(1, NX * NC)
    def _(step):
        greet((wide, lax.rem(narrow + step, NX * NC)))

    for dy in range(1, NY):
        for dc in range(NC):
            greet(device(x, lax.rem(y + dy, NY), z, dc))

    h_lanes = hadamard(2 * LANES, LANES, 7)

    @pl.loop(0, outer // 8)
    def _(step):
        for sub in range(8):
            a = step * 8 + sub
            lanes = pl.ds(pl.multiple_of(a * LANES, LANES), LANES)
            row = signs[pl.ds(a, 1), :].astype(jnp.float32)
            mixed[pl.ds(pl.multiple_of(a * 8, 8), 8), :] = panel[:, lanes] * row

    @pl.loop(0, 8)
    def _(step):
        rows = pl.ds(pl.multiple_of(step * outer, outer), outer)
        high, low = split(mixed[rows, :])
        both = jnp.concatenate([high, low], axis=1)
        mixed[rows, :] = jnp.dot(both, h_lanes, preferred_element_type=jnp.float32)

    pl.semaphore_wait(barrier, NX * NC - 1 + (NY - 1) * NC + NZ - 1)

    def z_order(step):
        shift = jnp.where(step % 2 == 1, (step + 1) // 2, NZ - step // 2)
        return lax.rem(z + NZ // 2 + shift, NZ)

    idx_y[y, z] = samples[...]

    @pl.loop(0, NZ - 1)
    def _(step):
        remote(samples, idx_y.at[y, z], iz_send, iz_recv, device(x, y, z_order(step), core)).start()

    h_rows = hadamard(outer, outer, outer.bit_length() - 1)
    for j in range(8):
        high, low = split(mixed[pl.ds(j, outer, stride=8), :])
        both = jnp.concatenate([high, low], axis=1)
        done = jnp.dot(h_rows, both, preferred_element_type=jnp.float32)
        sent[j] = done[:, :LANES] + done[:, LANES:]
        if j < 4:
            to, slot = device(j, y, z, 0), x * NC + core
            mine = (core == 0) & (x == j)
        else:
            to, slot = device(x, j - 4, z, 1), y * NC + core
            mine = (core == 1) & (y == j - 4)

        @pl.when(mine)
        def _():
            pltpu.make_async_copy(sent.at[j], came.at[slot], local.at[0]).start()

        @pl.when(jnp.logical_not(mine))
        def _():
            remote(sent.at[j], came.at[slot], x_send, x_recv, to).start()

    wait_bytes(idx_y.at[0, pl.ds(0, NZ - 1)], iz_recv)
    keep = pltpu.make_async_copy(idx_y.at[y], idx_x.at[x], local.at[1])
    keep.start()
    for step in range(1, 4):
        to = device(x, lax.rem(y + step, NY), z, core)
        remote(idx_y.at[y], idx_y.at[y], iy_send, iy_recv, to).start()
        to = device(lax.rem(x + step, NX), y, z, core)
        remote(idx_y.at[y], idx_x.at[x], ix_send, ix_recv, to).start()
    keep.wait()
    wait_bytes(idx_y.at[pl.ds(0, 3)], iy_recv)
    wait_bytes(idx_y.at[pl.ds(0, 3)], ix_recv)
    for j in range(8):
        if j < 4:
            source, to, slot = idx_y, device(j, y, z, 0), x * NC + core
            mine = (core == 0) & (x == j)
        else:
            source, to, slot = idx_x, device(x, j - 4, z, 1), y * NC + core
            mine = (core == 1) & (y == j - 4)

        @pl.when(mine)
        def _():
            pltpu.make_async_copy(source, idx_all.at[slot], local.at[2]).start()

        @pl.when(jnp.logical_not(mine))
        def _():
            remote(source, idx_all.at[slot], ia_send, ia_recv, to).start()

    wait_bytes(came.at[0], local.at[0])
    wait_bytes(came.at[pl.ds(0, 7)], x_recv)

    @pl.loop(0, outer // 8)
    def _(step):
        rows = pl.ds(pl.multiple_of(step * 8, 8), 8)
        values = [came[m, rows, :] for m in range(8)]
        for level in range(3):
            half = 1 << level
            for m in range(8):
                if not m & half:
                    first, second = values[m], values[m | half]
                    values[m], values[m | half] = first + second, first - second
        for m in range(8):
            table[m, rows, :] = values[m]

    wait_bytes(idx_all.at[0], local.at[2])
    wait_bytes(idx_all.at[pl.ds(0, 7)], ia_recv)

    sublane = lax.broadcasted_iota(jnp.int32, (8, LANES), 0)

    def choose(step):
        to_z = z_order(step)

        @pl.loop(0, 4)
        def _(turn):
            to_q = lax.rem(q + 1 + turn, 4)

            @pl.loop(0, 8)
            def _(m):
                offset = jnp.broadcast_to(idx_all[m, to_q, to_z], (8, LANES)) & (outer * LANES - 1)
                lane = offset & (LANES - 1)
                key = (offset >> 7) - sublane
                found = jnp.zeros((8, LANES), jnp.float32)
                for i in range(outer // 8):
                    there = jnp.take_along_axis(
                        table[m, 8 * i : 8 * i + 8, :], lane, axis=1, mode="promise_in_bounds"
                    )
                    found = jnp.where(key == 8 * i, there, found)
                pick[to_z, turn, pl.ds(m, 1), :] = jnp.sum(found, axis=0, keepdims=True)

            @pl.when(turn < 3)
            def _():
                remote(
                    pick.at[to_z, turn], part.at[to_z, q], q_send, q_recv.at[to_z], by_role(p, to_q, z)
                ).start()

        part[to_z, q] = pick[to_z, 3]

    def pass_on(step):
        to_z = z_order(step)
        wait_bytes(part.at[0, pl.ds(0, 3)], q_recv.at[to_z])
        total = signed(parity(q & 0, 2), part[to_z, 0])
        for other in range(1, 4):
            total = total + signed(parity(q & other, 2), part[to_z, other])

        @pl.when(step < NZ - 1)
        def _():
            zsum[to_z] = total
            remote(zsum.at[to_z], zcame.at[z], z_send, z_recv, by_role(p, q, to_z)).start()

        @pl.when(step == NZ - 1)
        def _():
            zcame[z] = total

    @pl.loop(0, NZ)
    def _(step):
        choose(step)

        @pl.when(step >= LAG)
        def _():
            pass_on(step - LAG)

    @pl.loop(NZ - LAG, NZ)
    def _(step):
        pass_on(step)

    wait_bytes(zcame.at[pl.ds(0, NZ - 1)], z_recv)
    total = zcame[0]
    for other in range(1, NZ):
        total = total + signed(parity(z & other, 4), zcame[other])
    total = total * scale
    slot = core * 4 + p
    for m in range(8):
        rows_out[m] = total[m : m + 1, :]
    for m in range(8):
        to = device(jnp.where(role0, m // 2, x), jnp.where(role0, y, m // 2), z, m % 2)
        mine = (p == m // 2) & (core == m % 2)

        @pl.when(mine)
        def _():
            pltpu.make_async_copy(rows_out.at[m], rows_in.at[slot], local.at[3]).start()

        @pl.when(jnp.logical_not(mine))
        def _():
            remote(rows_out.at[m], rows_in.at[slot], r_send, r_recv, to).start()

    wait_bytes(rows_in.at[0], local.at[3])
    wait_bytes(rows_in.at[pl.ds(0, 7)], r_recv)
    for j in range(8):
        out[j : j + 1, :] = rows_in[j]

    wait_bytes(sent.at[pl.ds(0, 7)], x_send)
    wait_bytes(idx_y.at[0, pl.ds(0, NZ - 1)], iz_send)
    wait_bytes(idx_y.at[pl.ds(0, 3)], iy_send)
    wait_bytes(idx_y.at[pl.ds(0, 3)], ix_send)
    wait_bytes(idx_all.at[pl.ds(0, 7)], ia_send)
    wait_bytes(pick.at[pl.ds(0, 12)], q_send)
    wait_bytes(zsum.at[pl.ds(0, NZ - 1)], z_send)
    wait_bytes(rows_out.at[pl.ds(0, 7)], r_send)


def per_device(panel, signs, samples):
    cols, rows = panel.shape
    samp = samples.shape[0]
    n_wide, n_narrow = lax.axis_size("wide"), lax.axis_size("narrow")
    scale = 1.0 / math.sqrt(samp * n_wide * n_narrow)
    outer = rows // LANES
    dma = pltpu.SemaphoreType.DMA
    vmem = pl.BlockSpec(memory_space=pltpu.VMEM)
    f32, i32 = jnp.float32, jnp.int32
    return pl.pallas_call(
        functools.partial(kernel, scale),
        out_shape=jax.ShapeDtypeStruct((cols, samp), f32),
        in_specs=[vmem] * 3,
        out_specs=vmem,
        scratch_shapes=[
            pltpu.VMEM((cols * outer, LANES), f32),
            pltpu.VMEM((8, outer, LANES), f32),
            pltpu.VMEM((8, outer, LANES), f32),
            pltpu.VMEM((8, outer, LANES), f32),
            pltpu.VMEM((NY, NZ, 1, LANES), i32),
            pltpu.VMEM((NX, NZ, 1, LANES), i32),
            pltpu.VMEM((8, 4, NZ, 1, LANES), i32),
            pltpu.VMEM((NZ, 4, 8, LANES), f32),
            pltpu.VMEM((NZ, 4, 8, LANES), f32),
            pltpu.VMEM((NZ, 8, LANES), f32),
            pltpu.VMEM((NZ, 8, LANES), f32),
            pltpu.VMEM((8, 1, LANES), f32),
            pltpu.VMEM((8, 1, LANES), f32),
            dma, dma, dma, dma, dma, dma, dma, dma, dma, dma,
            dma, dma((NZ,)), dma, dma, dma, dma, dma((4,)),
        ],
        compiler_params=pltpu.CompilerParams(collective_id=0, has_side_effects=True),
    )(panel, signs.reshape(outer, LANES), samples.reshape(1, samp))


def solution(mesh):
    in_specs = (P(None, ("wide", "narrow")), P(("wide", "narrow")), P(("wide", "narrow")))
    out_specs = P(None, ("wide", "narrow"))
    return jax.shard_map(
        per_device, mesh=mesh, in_specs=in_specs, out_specs=out_specs, check_vma=False
    )
```

```python
import functools
import math

import jax
import jax.numpy as jnp
from jax import lax
from jax.experimental import pallas as pl
from jax.experimental.pallas import tpu as pltpu
from jax.sharding import PartitionSpec as P

MESH = pl.DeviceIdType.MESH
NX, NY, NZ, NC = 4, 4, 16, 2
LANES = 128
CHUNKS = 4
EARLY = 5


def parity(value, bits):
    shift = 1
    while shift * 2 < bits:
        shift *= 2
    while shift >= 1:
        value = value ^ (value >> shift)
        shift //= 2
    return value & 1


def hadamard(rows, columns, bits):
    left = lax.broadcasted_iota(jnp.int32, (rows, columns), 0)
    right = lax.broadcasted_iota(jnp.int32, (rows, columns), 1)
    odd = parity(left & right & ((1 << bits) - 1), bits)
    return (1 - 2 * odd).astype(jnp.float32).astype(jnp.bfloat16)


def split(values):
    high = values.astype(jnp.bfloat16)
    low = (values - high.astype(jnp.float32)).astype(jnp.bfloat16)
    return high, low


def signed(odd, values):
    return jnp.where(odd == 0, values, -values)


def kernel(
    scale, panel_hbm, signs_hbm, samples, out,
    panel, signs, mixed, sent, came, table, crossed, idx_z, idx_all, pick, zcame, rows_out, rows_in,
    load_sem, ring_send, up_recv, down_recv, x_send, x_recv, q_send, q_recv,
    i_send, i_recv, z_send, z_recv, r_send, r_recv,
):
    wide = lax.axis_index("wide")
    narrow = lax.axis_index("narrow")
    y, z = wide >> 4, wide & (NZ - 1)
    x, core = narrow >> 1, narrow & 1
    role0 = core == 0
    p = jnp.where(role0, x, y)
    q = jnp.where(role0, y, x)
    outer = signs_hbm.shape[0]
    rows_in_chunk = outer // CHUNKS

    def device(dx, dy, dz, dc):
        return (dy * NZ + dz, dx * NC + dc)

    def by_role(dp, dq, dz):
        return device(jnp.where(role0, dp, dq), jnp.where(role0, dq, dp), dz, core)

    def remote(src, dst, send, recv, to):
        return pltpu.make_async_remote_copy(
            src_ref=src, dst_ref=dst, send_sem=send, recv_sem=recv, device_id=to, device_id_type=MESH
        )

    def deliver(mine, src, dst, send, recv, to):
        @pl.when(mine)
        def _():
            pltpu.make_async_copy(src, dst, recv).start()

        @pl.when(jnp.logical_not(mine))
        def _():
            remote(src, dst, send, recv, to).start()

    def wait_bytes(ref, sem):
        pltpu.make_async_copy(ref, ref, sem).wait()

    def loads(chunk):
        lanes = pl.ds(chunk * rows_in_chunk * LANES, rows_in_chunk * LANES)
        rows = pl.ds(chunk * rows_in_chunk, rows_in_chunk)
        return (
            pltpu.make_async_copy(panel_hbm.at[:, lanes], panel.at[:, lanes], load_sem.at[chunk, 0]),
            pltpu.make_async_copy(signs_hbm.at[rows], signs.at[rows], load_sem.at[chunk, 1]),
        )

    for chunk in range(CHUNKS):
        for load in loads(chunk):
            load.start()

    barrier = pltpu.get_barrier_semaphore()

    def greet(to):
        pl.semaphore_signal(barrier, inc=1, device_id=to, device_id_type=MESH)

    above, below = (z + 1) & (NZ - 1), (z - 1) & (NZ - 1)
    greet(device(x, y, above, core))
    greet(device(x, y, below, core))

    @pl.loop(1, NX * NY * NC)
    def _(step):
        other = (narrow + y * NX * NC + step) & (NX * NY * NC - 1)
        greet(device((other >> 1) & 3, other >> 3, z, other & 1))

    h_lanes = hadamard(2 * LANES, LANES, 7)
    for chunk in range(CHUNKS):
        for load in loads(chunk):
            load.wait()
        flipped = []
        for sub in range(rows_in_chunk):
            a = chunk * rows_in_chunk + sub
            row = jnp.broadcast_to(signs[pl.ds(a, 1), :], (8, LANES)).astype(jnp.float32)
            flipped.append(panel[:, a * LANES : (a + 1) * LANES] * row)
        high, low = split(jnp.concatenate(flipped, axis=0))
        both = jnp.concatenate([high, low], axis=1)
        mixed[chunk * rows_in_chunk * 8 : (chunk + 1) * rows_in_chunk * 8, :] = jnp.dot(
            both, h_lanes, preferred_element_type=jnp.float32
        )
    h_rows = hadamard(outer, outer, outer.bit_length() - 1)

    pl.semaphore_wait(barrier, NX * NY * NC + 1)

    up, down = device(x, y, above, core), device(x, y, below, core)
    idx_z[z] = samples[...]

    def ring_up(step):
        row = (z - step) & (NZ - 1)
        src = samples if step == 0 else idx_z.at[row]
        return remote(src, idx_z.at[row], ring_send, up_recv.at[step], up)

    def ring_down(step):
        row = (z + step) & (NZ - 1)
        src = samples if step == 0 else idx_z.at[row]
        return remote(src, idx_z.at[row], ring_send, down_recv.at[step], down)

    def ring(step):
        ring_up(step - 1).wait_recv()
        if step < NZ // 2:
            ring_up(step).start()
            ring_down(step - 1).wait_recv()
            if step < NZ // 2 - 1:
                ring_down(step).start()

    ring_up(0).start()
    ring_down(0).start()

    for j in range(8):
        high, low = split(mixed[pl.ds(j, outer, stride=8), :])
        both = jnp.concatenate([high, low], axis=1)
        done = jnp.dot(h_rows, both, preferred_element_type=jnp.float32)
        sent[j] = done[:, :LANES] + done[:, LANES:]
        if j < 4:
            to, slot = device(j, y, z, 0), x * NC + core
            mine = (core == 0) & (x == j)
        else:
            to, slot = device(x, j - 4, z, 1), y * NC + core
            mine = (core == 1) & (y == j - 4)
        deliver(mine, sent.at[j], came.at[slot], x_send, x_recv, to)

    for step in range(1, EARLY + 1):
        ring(step)

    wait_bytes(came, x_recv)

    @pl.loop(0, outer // 8)
    def _(step):
        rows = pl.ds(pl.multiple_of(step * 8, 8), 8)
        values = [came[m, rows, :] for m in range(8)]
        for level in range(3):
            half = 1 << level
            for m in range(8):
                if not m & half:
                    first, second = values[m], values[m | half]
                    values[m], values[m | half] = first + second, first - second
        for m in range(8):
            table[m, rows, :] = values[m]

    for c in range(NC):
        for step in range(1, 4):
            to_q = (q + step) & 3
            remote(
                table.at[to_q * 2 + c], crossed.at[c, q], q_send, q_recv.at[c], by_role(p, to_q, z)
            ).start()
        pltpu.make_async_copy(table.at[q * 2 + c], crossed.at[c, q], q_recv.at[c]).start()

    for step in range(EARLY + 1, NZ // 2 + 1):
        ring(step)

    for i in range(4):
        deliver(
            role0 & (x == y) & (x == i), idx_z, idx_all.at[core, y], i_send, i_recv, device(i, x, z, 0)
        )
        deliver(
            (core == 1) & (x == y) & (y == i), idx_z, idx_all.at[core, x], i_send, i_recv, device(y, i, z, 1)
        )
    wait_bytes(idx_all, i_recv)

    sublane = lax.broadcasted_iota(jnp.int32, (8, LANES), 0)

    def fold_rows(groups):
        for level in (4, 2, 1):
            count = len(groups) // 2
            groups = [
                jnp.where(
                    (sublane & level) == 0,
                    first + pltpu.roll(first, 8 - level, 0),
                    second + pltpu.roll(second, level, 0),
                )
                for first, second in zip(groups[:count], groups[count:])
            ]
        return groups[0]

    def z_order(step):
        half = (step + 1) >> 1
        return (z + NZ // 2 + jnp.where((step & 1) == 1, half, NZ - half)) & (NZ - 1)

    for c in range(NC):
        wait_bytes(crossed.at[c], q_recv.at[c])

        @pl.loop(0, outer // 8)
        def _(step):
            rows = pl.ds(pl.multiple_of(step * 8, 8), 8)
            values = [crossed[c, m, rows, :] for m in range(4)]
            for level in range(2):
                half = 1 << level
                for m in range(4):
                    if not m & half:
                        first, second = values[m], values[m | half]
                        values[m], values[m | half] = first + second, first - second
            for m in range(4):
                came[c * 4 + m, rows, :] = values[m]

    @pl.loop(0, NZ)
    def _(step):
        to_z = z_order(step)
        found = []
        for m in range(8):
            offset = jnp.broadcast_to(idx_all[m // 4, m % 4, to_z], (8, LANES))
            lane = offset & (LANES - 1)
            key = ((offset >> 7) & (outer - 1)) - sublane
            chains = [jnp.zeros((8, LANES), jnp.float32)] * 2
            for i in range(outer // 8):
                there = jnp.take_along_axis(
                    came[m, 8 * i : 8 * i + 8, :], lane, axis=1, mode="promise_in_bounds"
                )
                chains[i & 1] = jnp.where(key == 8 * i, there, chains[i & 1])
            found.append(chains[0] + chains[1])
        pick[to_z] = fold_rows(found)

        @pl.when(step < NZ - 1)
        def _():
            remote(pick.at[to_z], zcame.at[z], z_send, z_recv, by_role(p, q, to_z)).start()

    zcame[z] = pick[z]
    wait_bytes(zcame.at[pl.ds(0, NZ - 1)], z_recv)
    total = zcame[0]
    for other in range(1, NZ):
        total = total + signed(parity(z & other, 4), zcame[other])
    total = total * scale
    for m in range(8):
        rows_out[m] = total[m : m + 1, :]
    slot = core * 4 + p
    for m in range(8):
        to_c, to_q = m // 4, m % 4
        to = device(jnp.where(role0, q, to_q), jnp.where(role0, to_q, q), z, to_c)
        mine = (core == to_c) & (p == q) & (q == to_q)
        deliver(mine, rows_out.at[m], rows_in.at[slot], r_send, r_recv, to)
    wait_bytes(rows_in, r_recv)
    for j in range(8):
        out[j : j + 1, :] = rows_in[j]

    wait_bytes(idx_z.at[pl.ds(0, NZ - 1)], ring_send)
    wait_bytes(sent.at[pl.ds(0, 7)], x_send)
    wait_bytes(sent.at[pl.ds(0, 6)], q_send)
    wait_bytes(pick.at[pl.ds(0, NZ - 1)], z_send)

    @pl.when(x == y)
    def _():
        wait_bytes(idx_all.at[0], i_send)
        wait_bytes(idx_all.at[0, pl.ds(0, 3)], i_send)
        wait_bytes(rows_out.at[pl.ds(0, 7)], r_send)

    @pl.when(x != y)
    def _():
        wait_bytes(idx_all, i_send)
        wait_bytes(rows_out, r_send)


def per_device(panel, signs, samples):
    cols, rows = panel.shape
    samp = samples.shape[0]
    n_wide, n_narrow = lax.axis_size("wide"), lax.axis_size("narrow")
    scale = 1.0 / math.sqrt(samp * n_wide * n_narrow)
    outer = rows // LANES
    dma = pltpu.SemaphoreType.DMA
    vmem = pl.BlockSpec(memory_space=pltpu.VMEM)
    hbm = pl.BlockSpec(memory_space=pl.ANY)
    f32, i32 = jnp.float32, jnp.int32
    return pl.pallas_call(
        functools.partial(kernel, scale),
        out_shape=jax.ShapeDtypeStruct((cols, samp), f32),
        in_specs=[hbm, hbm, vmem],
        out_specs=vmem,
        scratch_shapes=[
            pltpu.VMEM((cols, rows), f32),
            pltpu.VMEM((outer, LANES), i32),
            pltpu.VMEM((cols * outer, LANES), f32),
            pltpu.VMEM((8, outer, LANES), f32),
            pltpu.VMEM((8, outer, LANES), f32),
            pltpu.VMEM((8, outer, LANES), f32),
            pltpu.VMEM((NC, 4, outer, LANES), f32),
            pltpu.VMEM((NZ, 1, LANES), i32),
            pltpu.VMEM((NC, 4, NZ, 1, LANES), i32),
            pltpu.VMEM((NZ, 8, LANES), f32),
            pltpu.VMEM((NZ, 8, LANES), f32),
            pltpu.VMEM((8, 1, LANES), f32),
            pltpu.VMEM((8, 1, LANES), f32),
            dma((CHUNKS, 2)), dma, dma((NZ // 2,)), dma((NZ // 2,)), dma, dma, dma, dma((NC,)),
            dma, dma, dma, dma, dma, dma,
        ],
        compiler_params=pltpu.CompilerParams(collective_id=0, has_side_effects=True),
    )(panel, signs.reshape(outer, LANES), samples.reshape(1, samp))


def solution(mesh):
    in_specs = (P(None, ("wide", "narrow")), P(("wide", "narrow")), P(("wide", "narrow")))
    out_specs = P(None, ("wide", "narrow"))
    return jax.shard_map(
        per_device, mesh=mesh, in_specs=in_specs, out_specs=out_specs, check_vma=False
    )
```

```python
import functools
import math

import jax
import jax.numpy as jnp
from jax import lax
from jax.experimental import pallas as pl
from jax.experimental.pallas import tpu as pltpu
from jax.sharding import PartitionSpec as P

MESH = pl.DeviceIdType.MESH
NX, NY, NZ, NC = 4, 4, 16, 2
LANES = 128
CHUNKS = 4
HALVES = 2
NEAR = 4


def parity(value, bits):
    shift = 1
    while shift * 2 < bits:
        shift *= 2
    while shift >= 1:
        value = value ^ (value >> shift)
        shift //= 2
    return value & 1


def hadamard(rows, columns, bits):
    left = lax.broadcasted_iota(jnp.int32, (rows, columns), 0)
    right = lax.broadcasted_iota(jnp.int32, (rows, columns), 1)
    odd = parity(left & right & ((1 << bits) - 1), bits)
    return (1 - 2 * odd).astype(jnp.float32).astype(jnp.bfloat16)


def split(values):
    high = values.astype(jnp.bfloat16)
    low = (values - high.astype(jnp.float32)).astype(jnp.bfloat16)
    return high, low


def signed(odd, values):
    return jnp.where(odd == 0, values, -values)


def kernel(
    scale, panel_hbm, signs_hbm, samples, out,
    panel, signs, mixed, sent, came, table, crossed, idx_all, pick, zcame, rows_out, rows_in,
    load_sem, relay, x_send, x_recv, q_send, q_recv,
    ip_send, ip_recv, iz_send, iz_recv, z_send, z_recv, r_send, r_recv,
):
    wide = lax.axis_index("wide")
    narrow = lax.axis_index("narrow")
    y, z = wide >> 4, wide & (NZ - 1)
    x, core = narrow >> 1, narrow & 1
    role0 = core == 0
    p = jnp.where(role0, x, y)
    q = jnp.where(role0, y, x)
    outer = signs_hbm.shape[0]
    rows_in_chunk = outer // CHUNKS

    def device(dx, dy, dz, dc):
        return (dy * NZ + dz, dx * NC + dc)

    def by_role(dp, dq, dz):
        return device(jnp.where(role0, dp, dq), jnp.where(role0, dq, dp), dz, core)

    def remote(src, dst, send, recv, to):
        return pltpu.make_async_remote_copy(
            src_ref=src, dst_ref=dst, send_sem=send, recv_sem=recv, device_id=to, device_id_type=MESH
        )

    def deliver(mine, src, dst, send, recv, to):
        @pl.when(mine)
        def _():
            pltpu.make_async_copy(src, dst, recv).start()

        @pl.when(jnp.logical_not(mine))
        def _():
            remote(src, dst, send, recv, to).start()

    def wait_bytes(ref, sem):
        pltpu.make_async_copy(ref, ref, sem).wait()

    def loads(chunk):
        lanes = pl.ds(chunk * rows_in_chunk * LANES, rows_in_chunk * LANES)
        rows = pl.ds(chunk * rows_in_chunk, rows_in_chunk)
        return (
            pltpu.make_async_copy(panel_hbm.at[:, lanes], panel.at[:, lanes], load_sem.at[chunk, 0]),
            pltpu.make_async_copy(signs_hbm.at[rows], signs.at[rows], load_sem.at[chunk, 1]),
        )

    for chunk in range(CHUNKS):
        for load in loads(chunk):
            load.start()

    barrier = pltpu.get_barrier_semaphore()

    def greet(to):
        pl.semaphore_signal(barrier, inc=1, device_id=to, device_id_type=MESH)

    for step in range(1, NEAR + 1):
        greet(device(x, y, (z + step) & (NZ - 1), core))
        greet(device(x, y, (z - step) & (NZ - 1), core))

    @pl.loop(1, NX * NY * NC)
    def _(step):
        other = (narrow + y * NX * NC + step) & (NX * NY * NC - 1)
        greet(device((other >> 1) & 3, other >> 3, z, other & 1))

    h_lanes = hadamard(2 * LANES, LANES, 7)
    for chunk in range(CHUNKS):
        for load in loads(chunk):
            load.wait()
        flipped = []
        for sub in range(rows_in_chunk):
            a = chunk * rows_in_chunk + sub
            row = jnp.broadcast_to(signs[pl.ds(a, 1), :], (8, LANES)).astype(jnp.float32)
            flipped.append(panel[:, a * LANES : (a + 1) * LANES] * row)
        high, low = split(jnp.concatenate(flipped, axis=0))
        both = jnp.concatenate([high, low], axis=1)
        mixed[chunk * rows_in_chunk * 8 : (chunk + 1) * rows_in_chunk * 8, :] = jnp.dot(
            both, h_lanes, preferred_element_type=jnp.float32
        )
    h_rows = hadamard(outer, outer, outer.bit_length() - 1)

    for j in range(8):
        high, low = split(mixed[pl.ds(j, outer, stride=8), :])
        both = jnp.concatenate([high, low], axis=1)
        done = jnp.dot(h_rows, both, preferred_element_type=jnp.float32)
        sent[j] = done[:, :LANES] + done[:, LANES:]

    pl.semaphore_wait(barrier, NX * NY * NC - 1 + 2 * NEAR)

    for side, to_z in enumerate((z + NEAR, z - NEAR)):
        pl.semaphore_signal(
            relay.at[side], inc=1, device_id=device(x, y, to_z & (NZ - 1), core), device_id_type=MESH
        )

    for i in range(4):
        deliver(
            role0 & (x == y) & (x == i), samples, idx_all.at[z, core * 4 + y], ip_send, ip_recv,
            device(i, x, z, 0),
        )
        deliver(
            (core == 1) & (x == y) & (y == i), samples, idx_all.at[z, core * 4 + x], ip_send, ip_recv,
            device(y, i, z, 1),
        )

    for half in range(HALVES):
        rows = pl.ds(half * (outer // HALVES), outer // HALVES)

        def column(j, slot):
            return sent.at[j, rows], came.at[slot, rows]

        by_x, by_y = x * NC + core, y * NC + core
        for step in (2, 1, 3):
            other = (x + step) & 3
            remote(*column(other, by_x), x_send, x_recv.at[half], device(other, y, z, 0)).start()
            other = (y + step) & 3
            remote(*column(4 + other, by_y), x_send, x_recv.at[half], device(x, other, z, 1)).start()
        deliver(role0, *column(x, by_x), x_send, x_recv.at[half], device(x, y, z, 0))
        deliver(core == 1, *column(4 + y, by_y), x_send, x_recv.at[half], device(x, y, z, 1))

    def z_order(step):
        half = (step + 1) >> 1
        return (z + NZ // 2 + jnp.where((step & 1) == 1, half, NZ - half)) & (NZ - 1)

    pl.semaphore_wait(relay.at[0], 1)
    pl.semaphore_wait(relay.at[1], 1)
    wait_bytes(idx_all.at[0], ip_recv)

    @pl.loop(0, NZ - 1)
    def _(step):
        remote(idx_all.at[z], idx_all.at[z], iz_send, iz_recv, by_role(p, q, z_order(step))).start()

    for part in range(HALVES):
        wait_bytes(came.at[:, pl.ds(0, outer // HALVES)], x_recv.at[part])

        @pl.loop(part * (outer // 8 // HALVES), (part + 1) * (outer // 8 // HALVES))
        def _(step):
            rows = pl.ds(pl.multiple_of(step * 8, 8), 8)
            values = [came[m, rows, :] for m in range(8)]
            for level in range(3):
                half = 1 << level
                for m in range(8):
                    if not m & half:
                        first, second = values[m], values[m | half]
                        values[m], values[m | half] = first + second, first - second
            for m in range(8):
                table[m, rows, :] = values[m]

        rows = pl.ds(part * (outer // HALVES), outer // HALVES)
        for step in (2, 1, 3):
            to_q = (q + step) & 3
            for c in range(NC):
                remote(
                    table.at[to_q * 2 + c, rows], crossed.at[c, q, rows], q_send, q_recv.at[part],
                    by_role(p, to_q, z),
                ).start()
        for c in range(NC):
            pltpu.make_async_copy(
                table.at[q * 2 + c, rows], crossed.at[c, q, rows], q_recv.at[part]
            ).start()

    sublane = lax.broadcasted_iota(jnp.int32, (8, LANES), 0)

    def fold_rows(groups):
        for level in (4, 2, 1):
            count = len(groups) // 2
            groups = [
                jnp.where(
                    (sublane & level) == 0,
                    first + pltpu.roll(first, 8 - level, 0),
                    second + pltpu.roll(second, level, 0),
                )
                for first, second in zip(groups[:count], groups[count:])
            ]
        return groups[0]

    wait_bytes(idx_all.at[pl.ds(0, NZ - 1)], iz_recv)
    for part in range(HALVES):
        wait_bytes(crossed.at[:, :, pl.ds(0, outer // HALVES)], q_recv.at[part])

        @pl.loop(part * (outer // 8 // HALVES), (part + 1) * (outer // 8 // HALVES))
        def _(step):
            rows = pl.ds(pl.multiple_of(step * 8, 8), 8)
            for c in range(NC):
                values = [crossed[c, m, rows, :] for m in range(4)]
                for level in range(2):
                    half = 1 << level
                    for m in range(4):
                        if not m & half:
                            first, second = values[m], values[m | half]
                            values[m], values[m | half] = first + second, first - second
                for m in range(4):
                    came[c * 4 + m, rows, :] = values[m]

    @pl.loop(0, NZ)
    def _(step):
        to_z = z_order(step)
        found = []
        for m in range(8):
            offset = jnp.broadcast_to(idx_all[to_z, m], (8, LANES))
            lane = offset & (LANES - 1)
            key = ((offset >> 7) & (outer - 1)) - sublane
            chains = [jnp.zeros((8, LANES), jnp.float32)] * 2
            for i in range(outer // 8):
                there = jnp.take_along_axis(
                    came[m, 8 * i : 8 * i + 8, :], lane, axis=1, mode="promise_in_bounds"
                )
                chains[i & 1] = jnp.where(key == 8 * i, there, chains[i & 1])
            found.append(chains[0] + chains[1])
        pick[to_z] = fold_rows(found)

        @pl.when(step < NZ - 1)
        def _():
            remote(pick.at[to_z], zcame.at[z], z_send, z_recv, by_role(p, q, to_z)).start()

    zcame[z] = pick[z]
    wait_bytes(zcame.at[pl.ds(0, NZ - 1)], z_recv)
    total = zcame[0]
    for other in range(1, NZ):
        total = total + signed(parity(z & other, 4), zcame[other])
    total = total * scale
    for m in range(8):
        rows_out[m] = total[m : m + 1, :]
    slot = core * 4 + p
    for m in range(8):
        to_c, to_q = m // 4, m % 4
        to = device(jnp.where(role0, q, to_q), jnp.where(role0, to_q, q), z, to_c)
        mine = (core == to_c) & (p == q) & (q == to_q)
        deliver(mine, rows_out.at[m], rows_in.at[slot], r_send, r_recv, to)
    wait_bytes(rows_in, r_recv)
    for j in range(8):
        out[j : j + 1, :] = rows_in[j]

    wait_bytes(sent.at[pl.ds(0, 7)], x_send)
    wait_bytes(sent.at[pl.ds(0, 6)], q_send)
    wait_bytes(idx_all.at[pl.ds(0, NZ - 1)], iz_send)
    wait_bytes(pick.at[pl.ds(0, NZ - 1)], z_send)

    @pl.when(x == y)
    def _():
        wait_bytes(idx_all.at[0, pl.ds(0, 7)], ip_send)
        wait_bytes(rows_out.at[pl.ds(0, 7)], r_send)

    @pl.when(x != y)
    def _():
        wait_bytes(idx_all.at[0], ip_send)
        wait_bytes(rows_out, r_send)


def per_device(panel, signs, samples):
    cols, rows = panel.shape
    samp = samples.shape[0]
    n_wide, n_narrow = lax.axis_size("wide"), lax.axis_size("narrow")
    scale = 1.0 / math.sqrt(samp * n_wide * n_narrow)
    outer = rows // LANES
    dma = pltpu.SemaphoreType.DMA
    vmem = pl.BlockSpec(memory_space=pltpu.VMEM)
    hbm = pl.BlockSpec(memory_space=pl.ANY)
    f32, i32 = jnp.float32, jnp.int32
    return pl.pallas_call(
        functools.partial(kernel, scale),
        out_shape=jax.ShapeDtypeStruct((cols, samp), f32),
        in_specs=[hbm, hbm, hbm],
        out_specs=vmem,
        scratch_shapes=[
            pltpu.VMEM((cols, rows), f32),
            pltpu.VMEM((outer, LANES), i32),
            pltpu.VMEM((cols * outer, LANES), f32),
            pltpu.VMEM((8, outer, LANES), f32),
            pltpu.VMEM((8, outer, LANES), f32),
            pltpu.VMEM((8, outer, LANES), f32),
            pltpu.VMEM((NC, 4, outer, LANES), f32),
            pltpu.VMEM((NZ, 8, 1, LANES), i32),
            pltpu.VMEM((NZ, 8, LANES), f32),
            pltpu.VMEM((NZ, 8, LANES), f32),
            pltpu.VMEM((8, 1, LANES), f32),
            pltpu.VMEM((8, 1, LANES), f32),
            dma((CHUNKS, 2)), pltpu.SemaphoreType.REGULAR((2,)), dma, dma((HALVES,)), dma, dma((HALVES,)),
            dma, dma, dma, dma, dma, dma, dma, dma,
        ],
        compiler_params=pltpu.CompilerParams(collective_id=0, has_side_effects=True),
    )(panel, signs.reshape(outer, LANES), samples.reshape(1, samp))


def solution(mesh):
    in_specs = (P(None, ("wide", "narrow")), P(("wide", "narrow")), P(("wide", "narrow")))
    out_specs = P(None, ("wide", "narrow"))
    return jax.shard_map(
        per_device, mesh=mesh, in_specs=in_specs, out_specs=out_specs, check_vma=False
    )
```

```python
import functools
import math

import jax
import jax.numpy as jnp
from jax import lax
from jax.experimental import pallas as pl
from jax.experimental.pallas import tpu as pltpu
from jax.sharding import PartitionSpec as P

MESH = pl.DeviceIdType.MESH
NX, NY, NZ, NC = 4, 4, 16, 2
LANES = 128
CHUNKS = 4
HALVES = 2
NEAR = 4


def parity(value, bits):
    shift = 1
    while shift * 2 < bits:
        shift *= 2
    while shift >= 1:
        value = value ^ (value >> shift)
        shift //= 2
    return value & 1


def hadamard(rows, columns, bits):
    left = lax.broadcasted_iota(jnp.int32, (rows, columns), 0)
    right = lax.broadcasted_iota(jnp.int32, (rows, columns), 1)
    odd = parity(left & right & ((1 << bits) - 1), bits)
    return (1 - 2 * odd).astype(jnp.float32).astype(jnp.bfloat16)


def split(values):
    high = values.astype(jnp.bfloat16)
    low = (values - high.astype(jnp.float32)).astype(jnp.bfloat16)
    return high, low


def signed(odd, values):
    return jnp.where(odd == 0, values, -values)


def kernel(
    scale, panel_hbm, signs_hbm, samples, out,
    panel, signs, mixed, sent, came, table, crossed, idx_all, pick, zcame,
    load_sem, relay, x_send, x_recv, q_send, q_recv,
    ip_send, ip_recv, iz_send, iz_recv, z_send, z_recv,
):
    wide = lax.axis_index("wide")
    narrow = lax.axis_index("narrow")
    y, z = wide >> 4, wide & (NZ - 1)
    x, core = narrow >> 1, narrow & 1
    role0 = core == 0
    p = jnp.where(role0, x, y)
    q = jnp.where(role0, y, x)
    outer = signs_hbm.shape[0]
    rows_in_chunk = outer // CHUNKS

    def device(dx, dy, dz, dc):
        return (dy * NZ + dz, dx * NC + dc)

    def by_role(dp, dq, dz):
        return device(jnp.where(role0, dp, dq), jnp.where(role0, dq, dp), dz, core)

    def remote(src, dst, send, recv, to):
        return pltpu.make_async_remote_copy(
            src_ref=src, dst_ref=dst, send_sem=send, recv_sem=recv, device_id=to, device_id_type=MESH
        )

    def deliver(mine, src, dst, send, recv, to):
        @pl.when(mine)
        def _():
            pltpu.make_async_copy(src, dst, recv).start()

        @pl.when(jnp.logical_not(mine))
        def _():
            remote(src, dst, send, recv, to).start()

    def wait_bytes(ref, sem):
        pltpu.make_async_copy(ref, ref, sem).wait()

    def loads(chunk):
        lanes = pl.ds(chunk * rows_in_chunk * LANES, rows_in_chunk * LANES)
        rows = pl.ds(chunk * rows_in_chunk, rows_in_chunk)
        return (
            pltpu.make_async_copy(panel_hbm.at[:, lanes], panel.at[:, lanes], load_sem.at[chunk, 0]),
            pltpu.make_async_copy(signs_hbm.at[rows], signs.at[rows], load_sem.at[chunk, 1]),
        )

    for chunk in range(CHUNKS):
        for load in loads(chunk):
            load.start()

    barrier = pltpu.get_barrier_semaphore()

    def greet(to):
        pl.semaphore_signal(barrier, inc=1, device_id=to, device_id_type=MESH)

    for step in range(1, NEAR + 1):
        greet(device(x, y, (z + step) & (NZ - 1), core))
        greet(device(x, y, (z - step) & (NZ - 1), core))

    @pl.loop(1, NX * NY * NC)
    def _(step):
        other = (narrow + y * NX * NC + step) & (NX * NY * NC - 1)
        greet(device((other >> 1) & 3, other >> 3, z, other & 1))

    h_lanes = hadamard(2 * LANES, LANES, 7)
    for chunk in range(CHUNKS):
        for load in loads(chunk):
            load.wait()
        flipped = []
        for sub in range(rows_in_chunk):
            a = chunk * rows_in_chunk + sub
            row = jnp.broadcast_to(signs[pl.ds(a, 1), :], (8, LANES)).astype(jnp.float32)
            flipped.append(panel[:, a * LANES : (a + 1) * LANES] * row)
        high, low = split(jnp.concatenate(flipped, axis=0))
        both = jnp.concatenate([high, low], axis=1)
        mixed[chunk * rows_in_chunk * 8 : (chunk + 1) * rows_in_chunk * 8, :] = jnp.dot(
            both, h_lanes, preferred_element_type=jnp.float32
        )
    h_rows = hadamard(outer, outer, outer.bit_length() - 1)

    for j in range(8):
        high, low = split(mixed[pl.ds(j, outer, stride=8), :])
        both = jnp.concatenate([high, low], axis=1)
        done = jnp.dot(h_rows, both, preferred_element_type=jnp.float32)
        sent[j] = done[:, :LANES] + done[:, LANES:]

    pl.semaphore_wait(barrier, NX * NY * NC - 1 + 2 * NEAR)

    for side, to_z in enumerate((z + NEAR, z - NEAR)):
        pl.semaphore_signal(
            relay.at[side], inc=1, device_id=device(x, y, to_z & (NZ - 1), core), device_id_type=MESH
        )

    for i in range(4):
        deliver(
            role0 & (x == y) & (x == i), samples, idx_all.at[z, core * 4 + y], ip_send, ip_recv,
            device(i, x, z, 0),
        )
        deliver(
            (core == 1) & (x == y) & (y == i), samples, idx_all.at[z, core * 4 + x], ip_send, ip_recv,
            device(y, i, z, 1),
        )

    for half in range(HALVES):
        rows = pl.ds(half * (outer // HALVES), outer // HALVES)

        def column(j, slot):
            return sent.at[j, rows], came.at[slot, rows]

        by_x, by_y = x * NC + core, y * NC + core
        for step in (2, 1, 3):
            other = (x + step) & 3
            remote(*column(other, by_x), x_send, x_recv.at[half], device(other, y, z, 0)).start()
            other = (y + step) & 3
            remote(*column(4 + other, by_y), x_send, x_recv.at[half], device(x, other, z, 1)).start()
        deliver(role0, *column(x, by_x), x_send, x_recv.at[half], device(x, y, z, 0))
        deliver(core == 1, *column(4 + y, by_y), x_send, x_recv.at[half], device(x, y, z, 1))

    def z_order(step):
        half = (step + 1) >> 1
        return (z + NZ // 2 + jnp.where((step & 1) == 1, half, NZ - half)) & (NZ - 1)

    pl.semaphore_wait(relay.at[0], 1)
    pl.semaphore_wait(relay.at[1], 1)
    wait_bytes(idx_all.at[0], ip_recv)

    @pl.loop(0, NZ - 1)
    def _(step):
        remote(idx_all.at[z], idx_all.at[z], iz_send, iz_recv, by_role(p, q, z_order(step))).start()

    for part in range(HALVES):
        wait_bytes(came.at[:, pl.ds(0, outer // HALVES)], x_recv.at[part])

        @pl.loop(part * (outer // 8 // HALVES), (part + 1) * (outer // 8 // HALVES))
        def _(step):
            rows = pl.ds(pl.multiple_of(step * 8, 8), 8)
            values = [came[m, rows, :] for m in range(8)]
            for level in range(3):
                half = 1 << level
                for m in range(8):
                    if not m & half:
                        first, second = values[m], values[m | half]
                        values[m], values[m | half] = first + second, first - second
            for m in range(8):
                table[m, rows, :] = values[m]

        rows = pl.ds(part * (outer // HALVES), outer // HALVES)
        for step in (2, 1, 3):
            to_q = (q + step) & 3
            for c in range(NC):
                remote(
                    table.at[to_q * 2 + c, rows], crossed.at[c, q, rows], q_send, q_recv.at[part],
                    by_role(p, to_q, z),
                ).start()
        for c in range(NC):
            pltpu.make_async_copy(
                table.at[q * 2 + c, rows], crossed.at[c, q, rows], q_recv.at[part]
            ).start()

    sublane = lax.broadcasted_iota(jnp.int32, (8, LANES), 0)

    def fold_rows(groups):
        for level in (4, 2, 1):
            count = len(groups) // 2
            groups = [
                jnp.where(
                    (sublane & level) == 0,
                    first + pltpu.roll(first, 8 - level, 0),
                    second + pltpu.roll(second, level, 0),
                )
                for first, second in zip(groups[:count], groups[count:])
            ]
        return groups[0]

    wait_bytes(idx_all.at[pl.ds(0, NZ - 1)], iz_recv)
    for part in range(HALVES):
        wait_bytes(crossed.at[:, :, pl.ds(0, outer // HALVES)], q_recv.at[part])

        @pl.loop(part * (outer // 8 // HALVES), (part + 1) * (outer // 8 // HALVES))
        def _(step):
            rows = pl.ds(pl.multiple_of(step * 8, 8), 8)
            for c in range(NC):
                values = [crossed[c, m, rows, :] for m in range(4)]
                for level in range(2):
                    half = 1 << level
                    for m in range(4):
                        if not m & half:
                            first, second = values[m], values[m | half]
                            values[m], values[m | half] = first + second, first - second
                for m in range(4):
                    came[c * 4 + m, rows, :] = values[m]

    def choose(to_z):
        found = []
        for m in range(8):
            offset = jnp.broadcast_to(idx_all[to_z, m], (8, LANES))
            lane = offset & (LANES - 1)
            row = offset >> 7
            bits = [(row & (8 << level)) != 0 for level in range((outer // 8).bit_length() - 1)]
            waiting = []
            for i in range(outer // 8):
                there = jnp.take_along_axis(
                    came[m, 8 * i : 8 * i + 8, :], lane, axis=1, mode="promise_in_bounds"
                )
                level = 0
                while waiting and waiting[-1][0] == level:
                    there = jnp.where(bits[level], there, waiting.pop()[1])
                    level += 1
                waiting.append((level, there))
            found.append(jnp.where((row & 7) == sublane, waiting[0][1], 0.0))
        rows = fold_rows(found)
        for m in range(8):
            pick[to_z, m] = rows[m : m + 1, :]

    slot = core * 4 + p

    def owner(m, to_z):
        to_c, to_q = m // 4, m % 4
        return device(jnp.where(role0, q, to_q), jnp.where(role0, to_q, q), to_z, to_c)

    @pl.loop(0, NZ - 1)
    def _(step):
        to_z = z_order(step)
        choose(to_z)
        for m in range(8):
            remote(pick.at[to_z, m], zcame.at[z, slot], z_send, z_recv, owner(m, to_z)).start()

    choose(z)
    for m in range(8):
        mine = (core == m // 4) & (p == q) & (q == m % 4)
        deliver(mine, pick.at[z, m], zcame.at[z, slot], z_send, z_recv, owner(m, z))

    wait_bytes(zcame, z_recv)
    for j in range(8):
        total = zcame[0, j]
        for other in range(1, NZ):
            total = total + signed(parity(z & other, 4), zcame[other, j])
        out[j : j + 1, :] = total * scale

    wait_bytes(sent.at[pl.ds(0, 7)], x_send)
    wait_bytes(sent.at[pl.ds(0, 6)], q_send)
    wait_bytes(idx_all.at[pl.ds(0, NZ - 1)], iz_send)

    @pl.when(x == y)
    def _():
        wait_bytes(idx_all.at[0, pl.ds(0, 7)], ip_send)
        wait_bytes(pick.at[pl.ds(0, NZ - 1)], z_send)
        wait_bytes(pick.at[0, pl.ds(0, 7)], z_send)

    @pl.when(x != y)
    def _():
        wait_bytes(idx_all.at[0], ip_send)
        wait_bytes(pick, z_send)


def per_device(panel, signs, samples):
    cols, rows = panel.shape
    samp = samples.shape[0]
    n_wide, n_narrow = lax.axis_size("wide"), lax.axis_size("narrow")
    scale = 1.0 / math.sqrt(samp * n_wide * n_narrow)
    outer = rows // LANES
    dma = pltpu.SemaphoreType.DMA
    vmem = pl.BlockSpec(memory_space=pltpu.VMEM)
    hbm = pl.BlockSpec(memory_space=pl.ANY)
    f32, i32 = jnp.float32, jnp.int32
    return pl.pallas_call(
        functools.partial(kernel, scale),
        out_shape=jax.ShapeDtypeStruct((cols, samp), f32),
        in_specs=[hbm, hbm, hbm],
        out_specs=vmem,
        scratch_shapes=[
            pltpu.VMEM((cols, rows), f32),
            pltpu.VMEM((outer, LANES), i32),
            pltpu.VMEM((cols * outer, LANES), f32),
            pltpu.VMEM((8, outer, LANES), f32),
            pltpu.VMEM((8, outer, LANES), f32),
            pltpu.VMEM((8, outer, LANES), f32),
            pltpu.VMEM((NC, 4, outer, LANES), f32),
            pltpu.VMEM((NZ, 8, 1, LANES), i32),
            pltpu.VMEM((NZ, 8, 1, LANES), f32),
            pltpu.VMEM((NZ, 8, 1, LANES), f32),
            dma((CHUNKS, 2)), pltpu.SemaphoreType.REGULAR((2,)), dma, dma((HALVES,)), dma, dma((HALVES,)),
            dma, dma, dma, dma, dma, dma,
        ],
        compiler_params=pltpu.CompilerParams(collective_id=0, has_side_effects=True),
    )(panel, signs.reshape(outer, LANES), samples.reshape(1, samp))


def solution(mesh):
    in_specs = (P(None, ("wide", "narrow")), P(("wide", "narrow")), P(("wide", "narrow")))
    out_specs = P(None, ("wide", "narrow"))
    return jax.shard_map(
        per_device, mesh=mesh, in_specs=in_specs, out_specs=out_specs, check_vma=False
    )
```

```python
import functools
import math

import jax
import jax.numpy as jnp
from jax import lax
from jax.experimental import pallas as pl
from jax.experimental.pallas import tpu as pltpu
from jax.sharding import PartitionSpec as P

MESH = pl.DeviceIdType.MESH
NX, NY, NZ, NC = 4, 4, 16, 2
LANES = 128
CHUNKS = 2
PARTS = 4
NEAR = 4


def parity(value, bits):
    shift = 1
    while shift * 2 < bits:
        shift *= 2
    while shift >= 1:
        value = value ^ (value >> shift)
        shift //= 2
    return value & 1


def hadamard(rows, columns, bits):
    left = lax.broadcasted_iota(jnp.int32, (rows, columns), 0)
    right = lax.broadcasted_iota(jnp.int32, (rows, columns), 1)
    odd = parity(left & right & ((1 << bits) - 1), bits)
    return (1 - 2 * odd).astype(jnp.float32).astype(jnp.bfloat16)


def split(values):
    high = values.astype(jnp.bfloat16)
    low = (values - high.astype(jnp.float32)).astype(jnp.bfloat16)
    return high, low


def signed(odd, values):
    return jnp.where(odd == 0, values, -values)


def kernel(
    scale, panel_hbm, signs_hbm, samples, out,
    panel, signs, mixed, sent, came, table, crossed, idx_all, pick, zcame,
    load_sem, relay, x_send, x_recv, q_send, q_recv,
    ip_send, ip_recv, iz_send, iz_recv, z_send, z_recv,
):
    wide = lax.axis_index("wide")
    narrow = lax.axis_index("narrow")
    y, z = wide >> 4, wide & (NZ - 1)
    x, core = narrow >> 1, narrow & 1
    role0 = core == 0
    p = jnp.where(role0, x, y)
    q = jnp.where(role0, y, x)
    outer = signs_hbm.shape[0]
    rows_in_chunk = outer // CHUNKS

    def device(dx, dy, dz, dc):
        return (dy * NZ + dz, dx * NC + dc)

    def by_role(dp, dq, dz):
        return device(jnp.where(role0, dp, dq), jnp.where(role0, dq, dp), dz, core)

    def remote(src, dst, send, recv, to):
        return pltpu.make_async_remote_copy(
            src_ref=src, dst_ref=dst, send_sem=send, recv_sem=recv, device_id=to, device_id_type=MESH
        )

    def deliver(mine, src, dst, send, recv, to):
        @pl.when(mine)
        def _():
            pltpu.make_async_copy(src, dst, recv).start()

        @pl.when(jnp.logical_not(mine))
        def _():
            remote(src, dst, send, recv, to).start()

    def wait_bytes(ref, sem):
        pltpu.make_async_copy(ref, ref, sem).wait()

    def loads(chunk):
        lanes = pl.ds(chunk * rows_in_chunk * LANES, rows_in_chunk * LANES)
        rows = pl.ds(chunk * rows_in_chunk, rows_in_chunk)
        return (
            pltpu.make_async_copy(panel_hbm.at[:, lanes], panel.at[:, lanes], load_sem.at[chunk, 0]),
            pltpu.make_async_copy(signs_hbm.at[rows], signs.at[rows], load_sem.at[chunk, 1]),
        )

    for chunk in range(CHUNKS):
        for load in loads(chunk):
            load.start()

    barrier = pltpu.get_barrier_semaphore()

    def greet(to):
        pl.semaphore_signal(barrier, inc=1, device_id=to, device_id_type=MESH)

    for step in range(1, NEAR + 1):
        greet(device(x, y, (z + step) & (NZ - 1), core))
        greet(device(x, y, (z - step) & (NZ - 1), core))

    @pl.loop(1, NX * NY * NC)
    def _(step):
        other = (narrow + y * NX * NC + step) & (NX * NY * NC - 1)
        greet(device((other >> 1) & 3, other >> 3, z, other & 1))

    h_lanes = hadamard(2 * LANES, LANES, 7)
    for chunk in range(CHUNKS):
        for load in loads(chunk):
            load.wait()
        flipped = []
        for sub in range(rows_in_chunk):
            a = chunk * rows_in_chunk + sub
            row = jnp.broadcast_to(signs[pl.ds(a, 1), :], (8, LANES)).astype(jnp.float32)
            flipped.append(panel[:, a * LANES : (a + 1) * LANES] * row)
        high, low = split(jnp.concatenate(flipped, axis=0))
        both = jnp.concatenate([high, low], axis=1)
        mixed[chunk * rows_in_chunk * 8 : (chunk + 1) * rows_in_chunk * 8, :] = jnp.dot(
            both, h_lanes, preferred_element_type=jnp.float32
        )
    h_rows = hadamard(outer, outer, outer.bit_length() - 1)

    for j in range(8):
        high, low = split(mixed[pl.ds(j, outer, stride=8), :])
        both = jnp.concatenate([high, low], axis=1)
        done = jnp.dot(h_rows, both, preferred_element_type=jnp.float32)
        sent[j] = done[:, :LANES] + done[:, LANES:]

    pl.semaphore_wait(barrier, NX * NY * NC - 1 + 2 * NEAR)

    for side, to_z in enumerate((z + NEAR, z - NEAR)):
        pl.semaphore_signal(
            relay.at[side], inc=1, device_id=device(x, y, to_z & (NZ - 1), core), device_id_type=MESH
        )

    for i in range(4):
        deliver(
            role0 & (x == y) & (x == i), samples, idx_all.at[z, core * 4 + y], ip_send, ip_recv,
            device(i, x, z, 0),
        )
        deliver(
            (core == 1) & (x == y) & (y == i), samples, idx_all.at[z, core * 4 + x], ip_send, ip_recv,
            device(y, i, z, 1),
        )

    for half in range(PARTS):
        rows = pl.ds(half * (outer // PARTS), outer // PARTS)

        def column(j, slot):
            return sent.at[j, rows], came.at[slot, rows]

        by_x, by_y = x * NC + core, y * NC + core
        for step in (2, 1, 3):
            other = (x + step) & 3
            remote(*column(other, by_x), x_send, x_recv.at[half], device(other, y, z, 0)).start()
            other = (y + step) & 3
            remote(*column(4 + other, by_y), x_send, x_recv.at[half], device(x, other, z, 1)).start()
        deliver(role0, *column(x, by_x), x_send, x_recv.at[half], device(x, y, z, 0))
        deliver(core == 1, *column(4 + y, by_y), x_send, x_recv.at[half], device(x, y, z, 1))

    def z_order(step):
        half = (step + 1) >> 1
        return (z + NZ // 2 + jnp.where((step & 1) == 1, half, NZ - half)) & (NZ - 1)

    pl.semaphore_wait(relay.at[0], 1)
    pl.semaphore_wait(relay.at[1], 1)
    wait_bytes(idx_all.at[0], ip_recv)

    @pl.loop(0, NZ - 1)
    def _(step):
        remote(idx_all.at[z], idx_all.at[z], iz_send, iz_recv, by_role(p, q, z_order(step))).start()

    for part in range(PARTS):
        wait_bytes(came.at[:, pl.ds(0, outer // PARTS)], x_recv.at[part])

        @pl.loop(part * (outer // 8 // PARTS), (part + 1) * (outer // 8 // PARTS))
        def _(step):
            rows = pl.ds(pl.multiple_of(step * 8, 8), 8)
            values = [came[m, rows, :] for m in range(8)]
            for level in range(3):
                half = 1 << level
                for m in range(8):
                    if not m & half:
                        first, second = values[m], values[m | half]
                        values[m], values[m | half] = first + second, first - second
            for m in range(8):
                table[m, rows, :] = values[m]

        rows = pl.ds(part * (outer // PARTS), outer // PARTS)
        for step in (2, 1, 3):
            to_q = (q + step) & 3
            for c in range(NC):
                remote(
                    table.at[to_q * 2 + c, rows], crossed.at[c, q, rows], q_send, q_recv.at[part],
                    by_role(p, to_q, z),
                ).start()
        for c in range(NC):
            pltpu.make_async_copy(
                table.at[q * 2 + c, rows], crossed.at[c, q, rows], q_recv.at[part]
            ).start()

    sublane = lax.broadcasted_iota(jnp.int32, (8, LANES), 0)

    def fold_rows(groups):
        for level in (4, 2, 1):
            count = len(groups) // 2
            groups = [
                jnp.where(
                    (sublane & level) == 0,
                    first + pltpu.roll(first, 8 - level, 0),
                    second + pltpu.roll(second, level, 0),
                )
                for first, second in zip(groups[:count], groups[count:])
            ]
        return groups[0]

    wait_bytes(idx_all.at[pl.ds(0, NZ - 1)], iz_recv)
    for part in range(PARTS):
        wait_bytes(crossed.at[:, :, pl.ds(0, outer // PARTS)], q_recv.at[part])

        @pl.loop(part * (outer // 8 // PARTS), (part + 1) * (outer // 8 // PARTS))
        def _(step):
            rows = pl.ds(pl.multiple_of(step * 8, 8), 8)
            for c in range(NC):
                values = [crossed[c, m, rows, :] for m in range(4)]
                for level in range(2):
                    half = 1 << level
                    for m in range(4):
                        if not m & half:
                            first, second = values[m], values[m | half]
                            values[m], values[m | half] = first + second, first - second
                for m in range(4):
                    came[c * 4 + m, rows, :] = values[m]

    def choose(to_z):
        found = []
        for m in range(8):
            offset = jnp.broadcast_to(idx_all[to_z, m], (8, LANES))
            lane = offset & (LANES - 1)
            row = offset >> 7
            bits = [(row & (8 << level)) != 0 for level in range((outer // 8).bit_length() - 1)]
            waiting = []
            for i in range(outer // 8):
                there = jnp.take_along_axis(
                    came[m, 8 * i : 8 * i + 8, :], lane, axis=1, mode="promise_in_bounds"
                )
                level = 0
                while waiting and waiting[-1][0] == level:
                    there = jnp.where(bits[level], there, waiting.pop()[1])
                    level += 1
                waiting.append((level, there))
            found.append(jnp.where((row & 7) == sublane, waiting[0][1], 0.0))
        rows = fold_rows(found)
        for m in range(8):
            pick[to_z, m] = rows[m : m + 1, :]

    slot = core * 4 + p

    def owner(m, to_z):
        to_c, to_q = m // 4, m % 4
        return device(jnp.where(role0, q, to_q), jnp.where(role0, to_q, q), to_z, to_c)

    @pl.loop(0, NZ - 1)
    def _(step):
        to_z = z_order(step)
        choose(to_z)
        for m in range(8):
            remote(pick.at[to_z, m], zcame.at[z, slot], z_send, z_recv, owner(m, to_z)).start()

    choose(z)
    for m in range(8):
        mine = (core == m // 4) & (p == q) & (q == m % 4)
        deliver(mine, pick.at[z, m], zcame.at[z, slot], z_send, z_recv, owner(m, z))

    wait_bytes(zcame, z_recv)
    for j in range(8):
        total = zcame[0, j]
        for other in range(1, NZ):
            total = total + signed(parity(z & other, 4), zcame[other, j])
        out[j : j + 1, :] = total * scale

    wait_bytes(sent.at[pl.ds(0, 7)], x_send)
    wait_bytes(sent.at[pl.ds(0, 6)], q_send)
    wait_bytes(idx_all.at[pl.ds(0, NZ - 1)], iz_send)

    @pl.when(x == y)
    def _():
        wait_bytes(idx_all.at[0, pl.ds(0, 7)], ip_send)
        wait_bytes(pick.at[pl.ds(0, NZ - 1)], z_send)
        wait_bytes(pick.at[0, pl.ds(0, 7)], z_send)

    @pl.when(x != y)
    def _():
        wait_bytes(idx_all.at[0], ip_send)
        wait_bytes(pick, z_send)


def per_device(panel, signs, samples):
    cols, rows = panel.shape
    samp = samples.shape[0]
    n_wide, n_narrow = lax.axis_size("wide"), lax.axis_size("narrow")
    scale = 1.0 / math.sqrt(samp * n_wide * n_narrow)
    outer = rows // LANES
    dma = pltpu.SemaphoreType.DMA
    vmem = pl.BlockSpec(memory_space=pltpu.VMEM)
    hbm = pl.BlockSpec(memory_space=pl.ANY)
    f32, i32 = jnp.float32, jnp.int32
    return pl.pallas_call(
        functools.partial(kernel, scale),
        out_shape=jax.ShapeDtypeStruct((cols, samp), f32),
        in_specs=[hbm, hbm, hbm],
        out_specs=vmem,
        scratch_shapes=[
            pltpu.VMEM((cols, rows), f32),
            pltpu.VMEM((outer, LANES), i32),
            pltpu.VMEM((cols * outer, LANES), f32),
            pltpu.VMEM((8, outer, LANES), f32),
            pltpu.VMEM((8, outer, LANES), f32),
            pltpu.VMEM((8, outer, LANES), f32),
            pltpu.VMEM((NC, 4, outer, LANES), f32),
            pltpu.VMEM((NZ, 8, 1, LANES), i32),
            pltpu.VMEM((NZ, 8, 1, LANES), f32),
            pltpu.VMEM((NZ, 8, 1, LANES), f32),
            dma((CHUNKS, 2)), pltpu.SemaphoreType.REGULAR((2,)), dma, dma((PARTS,)), dma, dma((PARTS,)),
            dma, dma, dma, dma, dma, dma,
        ],
        compiler_params=pltpu.CompilerParams(collective_id=0, has_side_effects=True),
    )(panel, signs.reshape(outer, LANES), samples.reshape(1, samp))


def solution(mesh):
    in_specs = (P(None, ("wide", "narrow")), P(("wide", "narrow")), P(("wide", "narrow")))
    out_specs = P(None, ("wide", "narrow"))
    return jax.shard_map(
        per_device, mesh=mesh, in_specs=in_specs, out_specs=out_specs, check_vma=False
    )
```

```python
import math

import jax
import jax.numpy as jnp
from jax import lax
from jax.experimental import pallas as pl
from jax.experimental.pallas import tpu as pltpu
from jax.sharding import PartitionSpec as P

MESH = pl.DeviceIdType.MESH
NX, NY, NZ, NC = 4, 4, 16, 2
LANES = 128
CHUNKS = 2
PARTS = 4
NEAR = 4


def parity(value, bits):
    shift = 1
    while shift * 2 < bits:
        shift *= 2
    while shift >= 1:
        value = value ^ (value >> shift)
        shift //= 2
    return value & 1


def hadamard(rows, columns, bits):
    left = lax.broadcasted_iota(jnp.int32, (rows, columns), 0)
    right = lax.broadcasted_iota(jnp.int32, (rows, columns), 1)
    odd = parity(left & right & ((1 << bits) - 1), bits)
    return (1 - 2 * odd).astype(jnp.float32).astype(jnp.bfloat16)


def split(values):
    high = values.astype(jnp.bfloat16)
    low = (values - high.astype(jnp.float32)).astype(jnp.bfloat16)
    return high, low


def signed(odd, values):
    return jnp.where(odd == 0, values, -values)


def kernel(
    panel_hbm, signs_hbm, samples, out,
    panel, signs, mixed, sent, came, table, crossed, idx_all, pick, zcame,
    load_sem, relay, x_send, x_recv, q_send, q_recv,
    ip_send, ip_recv, iz_send, iz_recv, z_send, z_recv,
):
    wide = lax.axis_index("wide")
    narrow = lax.axis_index("narrow")
    y, z = wide >> 4, wide & (NZ - 1)
    x, core = narrow >> 1, narrow & 1
    role0 = core == 0
    p = jnp.where(role0, x, y)
    q = jnp.where(role0, y, x)
    outer = signs_hbm.shape[0]
    rows_in_chunk = outer // CHUNKS

    def device(dx, dy, dz, dc):
        return (dy * NZ + dz, dx * NC + dc)

    def by_role(dp, dq, dz):
        return device(jnp.where(role0, dp, dq), jnp.where(role0, dq, dp), dz, core)

    def remote(src, dst, send, recv, to):
        return pltpu.make_async_remote_copy(
            src_ref=src, dst_ref=dst, send_sem=send, recv_sem=recv, device_id=to, device_id_type=MESH
        )

    def deliver(mine, src, dst, send, recv, to):
        @pl.when(mine)
        def _():
            pltpu.make_async_copy(src, dst, recv).start()

        @pl.when(jnp.logical_not(mine))
        def _():
            remote(src, dst, send, recv, to).start()

    def wait_bytes(ref, sem):
        pltpu.make_async_copy(ref, ref, sem).wait()

    def loads(chunk):
        lanes = pl.ds(chunk * rows_in_chunk * LANES, rows_in_chunk * LANES)
        rows = pl.ds(chunk * rows_in_chunk, rows_in_chunk)
        return (
            pltpu.make_async_copy(panel_hbm.at[:, lanes], panel.at[:, lanes], load_sem.at[chunk, 0]),
            pltpu.make_async_copy(signs_hbm.at[rows], signs.at[rows], load_sem.at[chunk, 1]),
        )

    for chunk in range(CHUNKS):
        for load in loads(chunk):
            load.start()

    barrier = pltpu.get_barrier_semaphore()

    def greet(to):
        pl.semaphore_signal(barrier, inc=1, device_id=to, device_id_type=MESH)

    for step in range(1, NEAR + 1):
        greet(device(x, y, (z + step) & (NZ - 1), core))
        greet(device(x, y, (z - step) & (NZ - 1), core))

    @pl.loop(1, NX * NY * NC)
    def _(step):
        other = (narrow + y * NX * NC + step) & (NX * NY * NC - 1)
        greet(device((other >> 1) & 3, other >> 3, z, other & 1))

    h_lanes = hadamard(2 * LANES, LANES, 7)
    for chunk in range(CHUNKS):
        for load in loads(chunk):
            load.wait()
        flipped = []
        for sub in range(rows_in_chunk):
            a = chunk * rows_in_chunk + sub
            row = jnp.broadcast_to(signs[pl.ds(a, 1), :], (8, LANES)).astype(jnp.float32)
            flipped.append(panel[:, a * LANES : (a + 1) * LANES] * row)
        high, low = split(jnp.concatenate(flipped, axis=0))
        both = jnp.concatenate([high, low], axis=1)
        mixed[chunk * rows_in_chunk * 8 : (chunk + 1) * rows_in_chunk * 8, :] = jnp.dot(
            both, h_lanes, preferred_element_type=jnp.float32
        )
    h_rows = hadamard(outer, outer, outer.bit_length() - 1)

    for j in range(8):
        high, low = split(mixed[pl.ds(j, outer, stride=8), :])
        both = jnp.concatenate([high, low], axis=1)
        done = jnp.dot(h_rows, both, preferred_element_type=jnp.float32)
        sent[j] = done[:, :LANES] + done[:, LANES:]

    pl.semaphore_wait(barrier, NX * NY * NC - 1 + 2 * NEAR)

    for side, to_z in enumerate((z + NEAR, z - NEAR)):
        pl.semaphore_signal(
            relay.at[side], inc=1, device_id=device(x, y, to_z & (NZ - 1), core), device_id_type=MESH
        )

    for i in range(4):
        deliver(
            role0 & (x == y) & (x == i), samples, idx_all.at[z, core * 4 + y], ip_send, ip_recv,
            device(i, x, z, 0),
        )
        deliver(
            (core == 1) & (x == y) & (y == i), samples, idx_all.at[z, core * 4 + x], ip_send, ip_recv,
            device(y, i, z, 1),
        )

    for half in range(PARTS):
        rows = pl.ds(half * (outer // PARTS), outer // PARTS)

        def column(j, slot):
            return sent.at[j, rows], came.at[slot, rows]

        by_x, by_y = x * NC + core, y * NC + core
        for step in (2, 1, 3):
            other = (x + step) & 3
            remote(*column(other, by_x), x_send, x_recv.at[half], device(other, y, z, 0)).start()
            other = (y + step) & 3
            remote(*column(4 + other, by_y), x_send, x_recv.at[half], device(x, other, z, 1)).start()
        deliver(role0, *column(x, by_x), x_send, x_recv.at[half], device(x, y, z, 0))
        deliver(core == 1, *column(4 + y, by_y), x_send, x_recv.at[half], device(x, y, z, 1))

    def z_order(step):
        half = (step + 1) >> 1
        return (z + NZ // 2 + jnp.where((step & 1) == 1, half, NZ - half)) & (NZ - 1)

    pl.semaphore_wait(relay.at[0], 1)
    pl.semaphore_wait(relay.at[1], 1)
    wait_bytes(idx_all.at[0], ip_recv)

    @pl.loop(0, NZ - 1)
    def _(step):
        remote(idx_all.at[z], idx_all.at[z], iz_send, iz_recv, by_role(p, q, z_order(step))).start()

    for part in range(PARTS):
        wait_bytes(came.at[:, pl.ds(0, outer // PARTS)], x_recv.at[part])

        @pl.loop(part * (outer // 8 // PARTS), (part + 1) * (outer // 8 // PARTS))
        def _(step):
            rows = pl.ds(pl.multiple_of(step * 8, 8), 8)
            values = [came[m, rows, :] for m in range(8)]
            for level in range(3):
                half = 1 << level
                for m in range(8):
                    if not m & half:
                        first, second = values[m], values[m | half]
                        values[m], values[m | half] = first + second, first - second
            for m in range(8):
                table[m, rows, :] = values[m]

        rows = pl.ds(part * (outer // PARTS), outer // PARTS)
        for step in (2, 1, 3):
            to_q = (q + step) & 3
            for c in range(NC):
                remote(
                    table.at[to_q * 2 + c, rows], crossed.at[c, q, rows], q_send, q_recv.at[part],
                    by_role(p, to_q, z),
                ).start()
        for c in range(NC):
            pltpu.make_async_copy(
                table.at[q * 2 + c, rows], crossed.at[c, q, rows], q_recv.at[part]
            ).start()

    sublane = lax.broadcasted_iota(jnp.int32, (8, LANES), 0)

    def fold_rows(groups):
        for level in (4, 2, 1):
            count = len(groups) // 2
            groups = [
                jnp.where(
                    (sublane & level) == 0,
                    first + pltpu.roll(first, 8 - level, 0),
                    second + pltpu.roll(second, level, 0),
                )
                for first, second in zip(groups[:count], groups[count:])
            ]
        return groups[0]

    wait_bytes(idx_all.at[pl.ds(0, NZ - 1)], iz_recv)
    for part in range(PARTS):
        wait_bytes(crossed.at[:, :, pl.ds(0, outer // PARTS)], q_recv.at[part])

        @pl.loop(part * (outer // 8 // PARTS), (part + 1) * (outer // 8 // PARTS))
        def _(step):
            rows = pl.ds(pl.multiple_of(step * 8, 8), 8)
            for c in range(NC):
                values = [crossed[c, m, rows, :] for m in range(4)]
                for level in range(2):
                    half = 1 << level
                    for m in range(4):
                        if not m & half:
                            first, second = values[m], values[m | half]
                            values[m], values[m | half] = first + second, first - second
                for m in range(4):
                    came[c * 4 + m, rows, :] = values[m]

    def choose(to_z):
        found = []
        for m in range(8):
            offset = jnp.broadcast_to(idx_all[to_z, m], (8, LANES))
            lane = offset & (LANES - 1)
            row = offset >> 7
            bits = [(row & (8 << level)) != 0 for level in range((outer // 8).bit_length() - 1)]
            waiting = []
            for i in range(outer // 8):
                there = jnp.take_along_axis(
                    came[m, 8 * i : 8 * i + 8, :], lane, axis=1, mode="promise_in_bounds"
                )
                level = 0
                while waiting and waiting[-1][0] == level:
                    there = jnp.where(bits[level], there, waiting.pop()[1])
                    level += 1
                waiting.append((level, there))
            found.append(jnp.where((row & 7) == sublane, waiting[0][1], 0.0))
        rows = fold_rows(found)
        for m in range(8):
            pick[to_z, m] = rows[m : m + 1, :]

    slot = core * 4 + p

    def owner(m, to_z):
        to_c, to_q = m // 4, m % 4
        return device(jnp.where(role0, q, to_q), jnp.where(role0, to_q, q), to_z, to_c)

    @pl.loop(0, NZ - 1)
    def _(step):
        to_z = z_order(step)
        choose(to_z)
        for m in range(8):
            remote(pick.at[to_z, m], zcame.at[z, slot], z_send, z_recv, owner(m, to_z)).start()

    choose(z)
    for m in range(8):
        mine = (core == m // 4) & (p == q) & (q == m % 4)
        deliver(mine, pick.at[z, m], zcame.at[z, slot], z_send, z_recv, owner(m, z))

    wait_bytes(zcame, z_recv)
    for j in range(8):
        total = zcame[0, j]
        for other in range(1, NZ):
            total = total + signed(parity(z & other, 4), zcame[other, j])
        out[j : j + 1, :] = total

    wait_bytes(sent.at[pl.ds(0, 7)], x_send)
    wait_bytes(sent.at[pl.ds(0, 6)], q_send)
    wait_bytes(idx_all.at[pl.ds(0, NZ - 1)], iz_send)

    @pl.when(x == y)
    def _():
        wait_bytes(idx_all.at[0, pl.ds(0, 7)], ip_send)
        wait_bytes(pick.at[pl.ds(0, NZ - 1)], z_send)
        wait_bytes(pick.at[0, pl.ds(0, 7)], z_send)

    @pl.when(x != y)
    def _():
        wait_bytes(idx_all.at[0], ip_send)
        wait_bytes(pick, z_send)


def per_device(panel, signs, samples):
    cols, rows = panel.shape
    samp = samples.shape[0]
    n_wide, n_narrow = lax.axis_size("wide"), lax.axis_size("narrow")
    scale = 1.0 / math.sqrt(samp * n_wide * n_narrow)
    outer = rows // LANES
    dma = pltpu.SemaphoreType.DMA
    vmem = pl.BlockSpec(memory_space=pltpu.VMEM)
    hbm = pl.BlockSpec(memory_space=pl.ANY)
    f32, i32 = jnp.float32, jnp.int32
    picked = pl.pallas_call(
        kernel,
        out_shape=pltpu.VMEM((cols, samp), f32),
        in_specs=[hbm, hbm, hbm],
        out_specs=vmem,
        scratch_shapes=[
            pltpu.VMEM((cols, rows), f32),
            pltpu.VMEM((outer, LANES), i32),
            pltpu.VMEM((cols * outer, LANES), f32),
            pltpu.VMEM((8, outer, LANES), f32),
            pltpu.VMEM((8, outer, LANES), f32),
            pltpu.VMEM((8, outer, LANES), f32),
            pltpu.VMEM((NC, 4, outer, LANES), f32),
            pltpu.VMEM((NZ, 8, 1, LANES), i32),
            pltpu.VMEM((NZ, 8, 1, LANES), f32),
            pltpu.VMEM((NZ, 8, 1, LANES), f32),
            dma((CHUNKS, 2)), pltpu.SemaphoreType.REGULAR((2,)), dma, dma((PARTS,)), dma, dma((PARTS,)),
            dma, dma, dma, dma, dma, dma,
        ],
        compiler_params=pltpu.CompilerParams(collective_id=0, has_side_effects=True),
    )(panel, signs.reshape(outer, LANES), samples.reshape(1, samp))
    return picked * jnp.float32(scale)


def solution(mesh):
    in_specs = (P(None, ("wide", "narrow")), P(("wide", "narrow")), P(("wide", "narrow")))
    out_specs = P(None, ("wide", "narrow"))
    return jax.shard_map(
        per_device, mesh=mesh, in_specs=in_specs, out_specs=out_specs, check_vma=False
    )
```

```python
import math

import jax
import jax.numpy as jnp
from jax import lax
from jax.experimental import pallas as pl
from jax.experimental.pallas import tpu as pltpu
from jax.sharding import PartitionSpec as P

MESH = pl.DeviceIdType.MESH
NX, NY, NZ, NC = 4, 4, 16, 2
LANES = 128
CHUNKS = 2
PARTS = 4
NEAR = 4


def parity(value, bits):
    shift = 1
    while shift * 2 < bits:
        shift *= 2
    while shift >= 1:
        value = value ^ (value >> shift)
        shift //= 2
    return value & 1


def hadamard(rows, columns, bits):
    left = lax.broadcasted_iota(jnp.int32, (rows, columns), 0)
    right = lax.broadcasted_iota(jnp.int32, (rows, columns), 1)
    odd = parity(left & right & ((1 << bits) - 1), bits)
    return (1 - 2 * odd).astype(jnp.float32).astype(jnp.bfloat16)


def split(values):
    high = values.astype(jnp.bfloat16)
    low = (values - high.astype(jnp.float32)).astype(jnp.bfloat16)
    return high, low


def signed(odd, values):
    return jnp.where(odd == 0, values, -values)


def kernel(
    panel_hbm, signs_hbm, samples, out,
    panel, signs, mixed, sent, came, table, crossed, idx_all, pick, zcame,
    load_sem, relay, x_send, x_recv, q_send, q_recv,
    ip_send, ip_recv, iz_send, iz_recv, z_send, z_recv,
):
    wide = lax.axis_index("wide")
    narrow = lax.axis_index("narrow")
    y, z = wide >> 4, wide & (NZ - 1)
    x, core = narrow >> 1, narrow & 1
    role0 = core == 0
    p = jnp.where(role0, x, y)
    q = jnp.where(role0, y, x)
    outer = signs_hbm.shape[0]
    rows_in_chunk = outer // CHUNKS

    def device(dx, dy, dz, dc):
        return (dy * NZ + dz, dx * NC + dc)

    def by_role(dp, dq, dz):
        return device(jnp.where(role0, dp, dq), jnp.where(role0, dq, dp), dz, core)

    def remote(src, dst, send, recv, to):
        return pltpu.make_async_remote_copy(
            src_ref=src, dst_ref=dst, send_sem=send, recv_sem=recv, device_id=to, device_id_type=MESH
        )

    def deliver(mine, src, dst, send, recv, to):
        @pl.when(mine)
        def _():
            pltpu.make_async_copy(src, dst, recv).start()

        @pl.when(jnp.logical_not(mine))
        def _():
            remote(src, dst, send, recv, to).start()

    def wait_bytes(ref, sem):
        pltpu.make_async_copy(ref, ref, sem).wait()

    def loads(chunk):
        lanes = pl.ds(chunk * rows_in_chunk * LANES, rows_in_chunk * LANES)
        rows = pl.ds(chunk * rows_in_chunk, rows_in_chunk)
        return (
            pltpu.make_async_copy(panel_hbm.at[:, lanes], panel.at[:, lanes], load_sem.at[chunk, 0]),
            pltpu.make_async_copy(signs_hbm.at[rows], signs.at[rows], load_sem.at[chunk, 1]),
        )

    barrier = pltpu.get_barrier_semaphore()

    def greet(to):
        pl.semaphore_signal(barrier, inc=1, device_id=to, device_id_type=MESH)

    for step in range(NEAR, 0, -1):
        greet(device(x, y, (z + step) & (NZ - 1), core))
        greet(device(x, y, (z - step) & (NZ - 1), core))

    for chunk in range(CHUNKS):
        for load in loads(chunk):
            load.start()

    @pl.loop(1, NX * NY * NC)
    def _(step):
        other = (narrow + y * NX * NC + step) & (NX * NY * NC - 1)
        greet(device((other >> 1) & 3, other >> 3, z, other & 1))

    h_lanes = hadamard(2 * LANES, LANES, 7)
    for chunk in range(CHUNKS):
        for load in loads(chunk):
            load.wait()
        flipped = []
        for sub in range(rows_in_chunk):
            a = chunk * rows_in_chunk + sub
            row = jnp.broadcast_to(signs[pl.ds(a, 1), :], (8, LANES)).astype(jnp.float32)
            flipped.append(panel[:, a * LANES : (a + 1) * LANES] * row)
        high, low = split(jnp.concatenate(flipped, axis=0))
        both = jnp.concatenate([high, low], axis=1)
        mixed[chunk * rows_in_chunk * 8 : (chunk + 1) * rows_in_chunk * 8, :] = jnp.dot(
            both, h_lanes, preferred_element_type=jnp.float32
        )
    h_rows = hadamard(outer, outer, outer.bit_length() - 1)

    for j in range(8):
        high, low = split(mixed[pl.ds(j, outer, stride=8), :])
        both = jnp.concatenate([high, low], axis=1)
        done = jnp.dot(h_rows, both, preferred_element_type=jnp.float32)
        sent[j] = done[:, :LANES] + done[:, LANES:]

    pl.semaphore_wait(barrier, NX * NY * NC - 1 + 2 * NEAR)

    for side, to_z in enumerate((z + NEAR, z - NEAR)):
        pl.semaphore_signal(
            relay.at[side], inc=1, device_id=device(x, y, to_z & (NZ - 1), core), device_id_type=MESH
        )

    for i in range(4):
        deliver(
            role0 & (x == y) & (x == i), samples, idx_all.at[z, core * 4 + y], ip_send, ip_recv,
            device(i, x, z, 0),
        )
        deliver(
            (core == 1) & (x == y) & (y == i), samples, idx_all.at[z, core * 4 + x], ip_send, ip_recv,
            device(y, i, z, 1),
        )

    for half in range(PARTS):
        rows = pl.ds(half * (outer // PARTS), outer // PARTS)

        def column(j, slot):
            return sent.at[j, rows], came.at[slot, rows]

        by_x, by_y = x * NC + core, y * NC + core
        for step in (2, 1, 3):
            other = (x + step) & 3
            remote(*column(other, by_x), x_send, x_recv.at[half], device(other, y, z, 0)).start()
            other = (y + step) & 3
            remote(*column(4 + other, by_y), x_send, x_recv.at[half], device(x, other, z, 1)).start()
        deliver(role0, *column(x, by_x), x_send, x_recv.at[half], device(x, y, z, 0))
        deliver(core == 1, *column(4 + y, by_y), x_send, x_recv.at[half], device(x, y, z, 1))

    def z_order(step):
        half = (step + 1) >> 1
        return (z + NZ // 2 + jnp.where((step & 1) == 1, half, NZ - half)) & (NZ - 1)

    pl.semaphore_wait(relay.at[0], 1)
    pl.semaphore_wait(relay.at[1], 1)
    wait_bytes(idx_all.at[0], ip_recv)

    @pl.loop(0, NZ - 1)
    def _(step):
        remote(idx_all.at[z], idx_all.at[z], iz_send, iz_recv, by_role(p, q, z_order(step))).start()

    for part in range(PARTS):
        wait_bytes(came.at[:, pl.ds(0, outer // PARTS)], x_recv.at[part])

        @pl.loop(part * (outer // 8 // PARTS), (part + 1) * (outer // 8 // PARTS))
        def _(step):
            rows = pl.ds(pl.multiple_of(step * 8, 8), 8)
            values = [came[m, rows, :] for m in range(8)]
            for level in range(3):
                half = 1 << level
                for m in range(8):
                    if not m & half:
                        first, second = values[m], values[m | half]
                        values[m], values[m | half] = first + second, first - second
            for m in range(8):
                table[m, rows, :] = values[m]

        rows = pl.ds(part * (outer // PARTS), outer // PARTS)
        for step in (2, 1, 3):
            to_q = (q + step) & 3
            for c in range(NC):
                remote(
                    table.at[to_q * 2 + c, rows], crossed.at[c, q, rows], q_send, q_recv.at[part],
                    by_role(p, to_q, z),
                ).start()
        for c in range(NC):
            pltpu.make_async_copy(
                table.at[q * 2 + c, rows], crossed.at[c, q, rows], q_recv.at[part]
            ).start()

    sublane = lax.broadcasted_iota(jnp.int32, (8, LANES), 0)

    def fold_rows(groups):
        for level in (4, 2, 1):
            count = len(groups) // 2
            groups = [
                jnp.where(
                    (sublane & level) == 0,
                    first + pltpu.roll(first, 8 - level, 0),
                    second + pltpu.roll(second, level, 0),
                )
                for first, second in zip(groups[:count], groups[count:])
            ]
        return groups[0]

    wait_bytes(idx_all.at[pl.ds(0, NZ - 1)], iz_recv)
    for part in range(PARTS):
        wait_bytes(crossed.at[:, :, pl.ds(0, outer // PARTS)], q_recv.at[part])

        @pl.loop(part * (outer // 8 // PARTS), (part + 1) * (outer // 8 // PARTS))
        def _(step):
            rows = pl.ds(pl.multiple_of(step * 8, 8), 8)
            for c in range(NC):
                values = [crossed[c, m, rows, :] for m in range(4)]
                for level in range(2):
                    half = 1 << level
                    for m in range(4):
                        if not m & half:
                            first, second = values[m], values[m | half]
                            values[m], values[m | half] = first + second, first - second
                for m in range(4):
                    came[c * 4 + m, rows, :] = values[m]

    def choose(to_z):
        found = []
        for m in range(8):
            offset = jnp.broadcast_to(idx_all[to_z, m], (8, LANES))
            lane = offset & (LANES - 1)
            row = offset >> 7
            bits = [(row & (8 << level)) != 0 for level in range((outer // 8).bit_length() - 1)]
            waiting = []
            for i in range(outer // 8):
                there = jnp.take_along_axis(
                    came[m, 8 * i : 8 * i + 8, :], lane, axis=1, mode="promise_in_bounds"
                )
                level = 0
                while waiting and waiting[-1][0] == level:
                    there = jnp.where(bits[level], there, waiting.pop()[1])
                    level += 1
                waiting.append((level, there))
            found.append(jnp.where((row & 7) == sublane, waiting[0][1], 0.0))
        rows = fold_rows(found)
        for m in range(8):
            pick[to_z, m] = rows[m : m + 1, :]

    slot = core * 4 + p

    def owner(m, to_z):
        to_c, to_q = m // 4, m % 4
        return device(jnp.where(role0, q, to_q), jnp.where(role0, to_q, q), to_z, to_c)

    @pl.loop(0, NZ - 1)
    def _(step):
        to_z = z_order(step)
        choose(to_z)
        for m in range(8):
            remote(pick.at[to_z, m], zcame.at[z, slot], z_send, z_recv, owner(m, to_z)).start()

    choose(z)
    for m in range(8):
        mine = (core == m // 4) & (p == q) & (q == m % 4)
        deliver(mine, pick.at[z, m], zcame.at[z, slot], z_send, z_recv, owner(m, z))

    wait_bytes(zcame, z_recv)
    for j in range(8):
        total = zcame[0, j]
        for other in range(1, NZ):
            total = total + signed(parity(z & other, 4), zcame[other, j])
        out[j : j + 1, :] = total

    wait_bytes(sent.at[pl.ds(0, 7)], x_send)
    wait_bytes(sent.at[pl.ds(0, 6)], q_send)
    wait_bytes(idx_all.at[pl.ds(0, NZ - 1)], iz_send)

    @pl.when(x == y)
    def _():
        wait_bytes(idx_all.at[0, pl.ds(0, 7)], ip_send)
        wait_bytes(pick.at[pl.ds(0, NZ - 1)], z_send)
        wait_bytes(pick.at[0, pl.ds(0, 7)], z_send)

    @pl.when(x != y)
    def _():
        wait_bytes(idx_all.at[0], ip_send)
        wait_bytes(pick, z_send)


def per_device(panel, signs, samples):
    cols, rows = panel.shape
    samp = samples.shape[0]
    n_wide, n_narrow = lax.axis_size("wide"), lax.axis_size("narrow")
    scale = 1.0 / math.sqrt(samp * n_wide * n_narrow)
    outer = rows // LANES
    dma = pltpu.SemaphoreType.DMA
    vmem = pl.BlockSpec(memory_space=pltpu.VMEM)
    hbm = pl.BlockSpec(memory_space=pl.ANY)
    f32, i32 = jnp.float32, jnp.int32
    picked = pl.pallas_call(
        kernel,
        out_shape=pltpu.VMEM((cols, samp), f32),
        in_specs=[hbm, hbm, hbm],
        out_specs=vmem,
        scratch_shapes=[
            pltpu.VMEM((cols, rows), f32),
            pltpu.VMEM((outer, LANES), i32),
            pltpu.VMEM((cols * outer, LANES), f32),
            pltpu.VMEM((8, outer, LANES), f32),
            pltpu.VMEM((8, outer, LANES), f32),
            pltpu.VMEM((8, outer, LANES), f32),
            pltpu.VMEM((NC, 4, outer, LANES), f32),
            pltpu.VMEM((NZ, 8, 1, LANES), i32),
            pltpu.VMEM((NZ, 8, 1, LANES), f32),
            pltpu.VMEM((NZ, 8, 1, LANES), f32),
            dma((CHUNKS, 2)), pltpu.SemaphoreType.REGULAR((2,)), dma, dma((PARTS,)), dma, dma((PARTS,)),
            dma, dma, dma, dma, dma, dma,
        ],
        compiler_params=pltpu.CompilerParams(collective_id=0, has_side_effects=True),
    )(panel, signs.reshape(outer, LANES), samples.reshape(1, samp))
    return picked * jnp.float32(scale)


def solution(mesh):
    in_specs = (P(None, ("wide", "narrow")), P(("wide", "narrow")), P(("wide", "narrow")))
    out_specs = P(None, ("wide", "narrow"))
    return jax.shard_map(
        per_device, mesh=mesh, in_specs=in_specs, out_specs=out_specs, check_vma=False
    )
```

```python
import math

import jax
import jax.numpy as jnp
from jax import lax
from jax.experimental import pallas as pl
from jax.experimental.pallas import tpu as pltpu
from jax.sharding import PartitionSpec as P

MESH = pl.DeviceIdType.MESH
NX, NY, NZ, NC = 4, 4, 16, 2
LANES = 128
CHUNKS = 1
PARTS = 4
NEAR = 4


def parity(value, bits):
    shift = 1
    while shift * 2 < bits:
        shift *= 2
    while shift >= 1:
        value = value ^ (value >> shift)
        shift //= 2
    return value & 1


def hadamard(rows, columns, bits):
    left = lax.broadcasted_iota(jnp.int32, (rows, columns), 0)
    right = lax.broadcasted_iota(jnp.int32, (rows, columns), 1)
    odd = parity(left & right & ((1 << bits) - 1), bits)
    return (1 - 2 * odd).astype(jnp.float32).astype(jnp.bfloat16)


def split(values):
    high = values.astype(jnp.bfloat16)
    low = (values - high.astype(jnp.float32)).astype(jnp.bfloat16)
    return high, low


def signed(odd, values):
    return jnp.where(odd == 0, values, -values)


def kernel(
    panel_hbm, signs_hbm, samples, out,
    panel, signs, mixed, sent, came, table, crossed, idx_all, pick, zcame,
    load_sem, relay, x_send, x_recv, q_send, q_recv,
    ip_send, ip_recv, iz_send, iz_recv, z_send, z_recv,
):
    wide = lax.axis_index("wide")
    narrow = lax.axis_index("narrow")
    y, z = wide >> 4, wide & (NZ - 1)
    x, core = narrow >> 1, narrow & 1
    role0 = core == 0
    p = jnp.where(role0, x, y)
    q = jnp.where(role0, y, x)
    outer = signs_hbm.shape[0]
    rows_in_chunk = outer // CHUNKS

    def device(dx, dy, dz, dc):
        return (dy * NZ + dz, dx * NC + dc)

    def by_role(dp, dq, dz):
        return device(jnp.where(role0, dp, dq), jnp.where(role0, dq, dp), dz, core)

    def remote(src, dst, send, recv, to):
        return pltpu.make_async_remote_copy(
            src_ref=src, dst_ref=dst, send_sem=send, recv_sem=recv, device_id=to, device_id_type=MESH
        )

    def deliver(mine, src, dst, send, recv, to):
        @pl.when(mine)
        def _():
            pltpu.make_async_copy(src, dst, recv).start()

        @pl.when(jnp.logical_not(mine))
        def _():
            remote(src, dst, send, recv, to).start()

    def wait_bytes(ref, sem):
        pltpu.make_async_copy(ref, ref, sem).wait()

    def loads(chunk):
        lanes = pl.ds(chunk * rows_in_chunk * LANES, rows_in_chunk * LANES)
        rows = pl.ds(chunk * rows_in_chunk, rows_in_chunk)
        return (
            pltpu.make_async_copy(panel_hbm.at[:, lanes], panel.at[:, lanes], load_sem.at[chunk, 0]),
            pltpu.make_async_copy(signs_hbm.at[rows], signs.at[rows], load_sem.at[chunk, 1]),
        )

    for chunk in range(CHUNKS):
        for load in loads(chunk):
            load.start()

    barrier = pltpu.get_barrier_semaphore()

    def greet(to):
        pl.semaphore_signal(barrier, inc=1, device_id=to, device_id_type=MESH)

    for step in range(1, NEAR + 1):
        greet(device(x, y, (z + step) & (NZ - 1), core))
        greet(device(x, y, (z - step) & (NZ - 1), core))

    @pl.loop(1, NX * NY * NC)
    def _(step):
        other = (narrow + y * NX * NC + step) & (NX * NY * NC - 1)
        greet(device((other >> 1) & 3, other >> 3, z, other & 1))

    h_lanes = hadamard(2 * LANES, LANES, 7)
    for chunk in range(CHUNKS):
        for load in loads(chunk):
            load.wait()
        flipped = []
        for sub in range(rows_in_chunk):
            a = chunk * rows_in_chunk + sub
            row = jnp.broadcast_to(signs[pl.ds(a, 1), :], (8, LANES)).astype(jnp.float32)
            flipped.append(panel[:, a * LANES : (a + 1) * LANES] * row)
        high, low = split(jnp.concatenate(flipped, axis=0))
        both = jnp.concatenate([high, low], axis=1)
        mixed[chunk * rows_in_chunk * 8 : (chunk + 1) * rows_in_chunk * 8, :] = jnp.dot(
            both, h_lanes, preferred_element_type=jnp.float32
        )
    h_rows = hadamard(outer, outer, outer.bit_length() - 1)

    for j in range(8):
        high, low = split(mixed[pl.ds(j, outer, stride=8), :])
        both = jnp.concatenate([high, low], axis=1)
        done = jnp.dot(h_rows, both, preferred_element_type=jnp.float32)
        sent[j] = done[:, :LANES] + done[:, LANES:]

    pl.semaphore_wait(barrier, NX * NY * NC - 1 + 2 * NEAR)

    for side, to_z in enumerate((z + NEAR, z - NEAR)):
        pl.semaphore_signal(
            relay.at[side], inc=1, device_id=device(x, y, to_z & (NZ - 1), core), device_id_type=MESH
        )

    for i in range(4):
        deliver(
            role0 & (x == y) & (x == i), samples, idx_all.at[z, core * 4 + y], ip_send, ip_recv,
            device(i, x, z, 0),
        )
        deliver(
            (core == 1) & (x == y) & (y == i), samples, idx_all.at[z, core * 4 + x], ip_send, ip_recv,
            device(y, i, z, 1),
        )

    for half in range(PARTS):
        rows = pl.ds(half * (outer // PARTS), outer // PARTS)

        def column(j, slot):
            return sent.at[j, rows], came.at[slot, rows]

        by_x, by_y = x * NC + core, y * NC + core
        for step in (2, 1, 3):
            other = (x + step) & 3
            remote(*column(other, by_x), x_send, x_recv.at[half], device(other, y, z, 0)).start()
            other = (y + step) & 3
            remote(*column(4 + other, by_y), x_send, x_recv.at[half], device(x, other, z, 1)).start()
        deliver(role0, *column(x, by_x), x_send, x_recv.at[half], device(x, y, z, 0))
        deliver(core == 1, *column(4 + y, by_y), x_send, x_recv.at[half], device(x, y, z, 1))

    def z_order(step):
        half = (step + 1) >> 1
        return (z + NZ // 2 + jnp.where((step & 1) == 1, half, NZ - half)) & (NZ - 1)

    pl.semaphore_wait(relay.at[0], 1)
    pl.semaphore_wait(relay.at[1], 1)
    wait_bytes(idx_all.at[0], ip_recv)

    @pl.loop(0, NZ - 1)
    def _(step):
        remote(idx_all.at[z], idx_all.at[z], iz_send, iz_recv, by_role(p, q, z_order(step))).start()

    for part in range(PARTS):
        wait_bytes(came.at[:, pl.ds(0, outer // PARTS)], x_recv.at[part])

        @pl.loop(part * (outer // 8 // PARTS), (part + 1) * (outer // 8 // PARTS))
        def _(step):
            rows = pl.ds(pl.multiple_of(step * 8, 8), 8)
            values = [came[m, rows, :] for m in range(8)]
            for level in range(3):
                half = 1 << level
                for m in range(8):
                    if not m & half:
                        first, second = values[m], values[m | half]
                        values[m], values[m | half] = first + second, first - second
            for m in range(8):
                table[m, rows, :] = values[m]

        rows = pl.ds(part * (outer // PARTS), outer // PARTS)
        for step in (2, 1, 3):
            to_q = (q + step) & 3
            for c in range(NC):
                remote(
                    table.at[to_q * 2 + c, rows], crossed.at[c, q, rows], q_send, q_recv.at[part],
                    by_role(p, to_q, z),
                ).start()
        for c in range(NC):
            pltpu.make_async_copy(
                table.at[q * 2 + c, rows], crossed.at[c, q, rows], q_recv.at[part]
            ).start()

    sublane = lax.broadcasted_iota(jnp.int32, (8, LANES), 0)

    def fold_rows(groups):
        for level in (4, 2, 1):
            count = len(groups) // 2
            groups = [
                jnp.where(
                    (sublane & level) == 0,
                    first + pltpu.roll(first, 8 - level, 0),
                    second + pltpu.roll(second, level, 0),
                )
                for first, second in zip(groups[:count], groups[count:])
            ]
        return groups[0]

    wait_bytes(idx_all.at[pl.ds(0, NZ - 1)], iz_recv)
    for part in range(PARTS):
        wait_bytes(crossed.at[:, :, pl.ds(0, outer // PARTS)], q_recv.at[part])

        @pl.loop(part * (outer // 8 // PARTS), (part + 1) * (outer // 8 // PARTS))
        def _(step):
            rows = pl.ds(pl.multiple_of(step * 8, 8), 8)
            for c in range(NC):
                values = [crossed[c, m, rows, :] for m in range(4)]
                for level in range(2):
                    half = 1 << level
                    for m in range(4):
                        if not m & half:
                            first, second = values[m], values[m | half]
                            values[m], values[m | half] = first + second, first - second
                for m in range(4):
                    came[c * 4 + m, rows, :] = values[m]

    def choose(to_z):
        found = []
        for m in range(8):
            offset = jnp.broadcast_to(idx_all[to_z, m], (8, LANES))
            lane = offset & (LANES - 1)
            row = offset >> 7
            bits = [(row & (8 << level)) != 0 for level in range((outer // 8).bit_length() - 1)]
            waiting = []
            for i in range(outer // 8):
                there = jnp.take_along_axis(
                    came[m, 8 * i : 8 * i + 8, :], lane, axis=1, mode="promise_in_bounds"
                )
                level = 0
                while waiting and waiting[-1][0] == level:
                    there = jnp.where(bits[level], there, waiting.pop()[1])
                    level += 1
                waiting.append((level, there))
            found.append(jnp.where((row & 7) == sublane, waiting[0][1], 0.0))
        rows = fold_rows(found)
        for m in range(8):
            pick[to_z, m] = rows[m : m + 1, :]

    slot = core * 4 + p

    def owner(m, to_z):
        to_c, to_q = m // 4, m % 4
        return device(jnp.where(role0, q, to_q), jnp.where(role0, to_q, q), to_z, to_c)

    @pl.loop(0, NZ - 1)
    def _(step):
        to_z = z_order(step)
        choose(to_z)
        for m in range(8):
            remote(pick.at[to_z, m], zcame.at[z, slot], z_send, z_recv, owner(m, to_z)).start()

    choose(z)
    for m in range(8):
        mine = (core == m // 4) & (p == q) & (q == m % 4)
        deliver(mine, pick.at[z, m], zcame.at[z, slot], z_send, z_recv, owner(m, z))

    wait_bytes(zcame, z_recv)
    for j in range(8):
        total = zcame[0, j]
        for other in range(1, NZ):
            total = total + signed(parity(z & other, 4), zcame[other, j])
        out[j : j + 1, :] = total

    wait_bytes(sent.at[pl.ds(0, 7)], x_send)
    wait_bytes(sent.at[pl.ds(0, 6)], q_send)
    wait_bytes(idx_all.at[pl.ds(0, NZ - 1)], iz_send)

    @pl.when(x == y)
    def _():
        wait_bytes(idx_all.at[0, pl.ds(0, 7)], ip_send)
        wait_bytes(pick.at[pl.ds(0, NZ - 1)], z_send)
        wait_bytes(pick.at[0, pl.ds(0, 7)], z_send)

    @pl.when(x != y)
    def _():
        wait_bytes(idx_all.at[0], ip_send)
        wait_bytes(pick, z_send)


def per_device(panel, signs, samples):
    cols, rows = panel.shape
    samp = samples.shape[0]
    n_wide, n_narrow = lax.axis_size("wide"), lax.axis_size("narrow")
    scale = 1.0 / math.sqrt(samp * n_wide * n_narrow)
    outer = rows // LANES
    dma = pltpu.SemaphoreType.DMA
    vmem = pl.BlockSpec(memory_space=pltpu.VMEM)
    hbm = pl.BlockSpec(memory_space=pl.ANY)
    f32, i32 = jnp.float32, jnp.int32
    picked = pl.pallas_call(
        kernel,
        out_shape=pltpu.VMEM((cols, samp), f32),
        in_specs=[hbm, hbm, hbm],
        out_specs=vmem,
        scratch_shapes=[
            pltpu.VMEM((cols, rows), f32),
            pltpu.VMEM((outer, LANES), i32),
            pltpu.VMEM((cols * outer, LANES), f32),
            pltpu.VMEM((8, outer, LANES), f32),
            pltpu.VMEM((8, outer, LANES), f32),
            pltpu.VMEM((8, outer, LANES), f32),
            pltpu.VMEM((NC, 4, outer, LANES), f32),
            pltpu.VMEM((NZ, 8, 1, LANES), i32),
            pltpu.VMEM((NZ, 8, 1, LANES), f32),
            pltpu.VMEM((NZ, 8, 1, LANES), f32),
            dma((CHUNKS, 2)), pltpu.SemaphoreType.REGULAR((2,)), dma, dma((PARTS,)), dma, dma((PARTS,)),
            dma, dma, dma, dma, dma, dma,
        ],
        compiler_params=pltpu.CompilerParams(collective_id=0, has_side_effects=True),
    )(panel, signs.reshape(outer, LANES), samples.reshape(1, samp))
    return picked * jnp.float32(scale)


def solution(mesh):
    in_specs = (P(None, ("wide", "narrow")), P(("wide", "narrow")), P(("wide", "narrow")))
    out_specs = P(None, ("wide", "narrow"))
    return jax.shard_map(
        per_device, mesh=mesh, in_specs=in_specs, out_specs=out_specs, check_vma=False
    )
```
